32 devices in a mesh: slab: 4 (over y, core), row: 2 (over x), col: 4 (over z).
Axes of the slice: x: 2, y: 2, z: 4, core: 2. Of those that a mesh axis runs over, the one named last changes fastest.
Arguments:
- reflection: bfloat16 [4, 4096, 4096], P('slab', 'row', 'col'), may hold values from -0.0625 to 0.0625
- transmission: bfloat16 [4, 4096, 4096], P('slab', 'row', 'col'), may hold values from -0.09375 to 0.09375
- shots: bfloat16 [4, 4096, 1024], P('slab', 'row', 'col'), may hold values from -6 to 6
Outputs:
- merged: bfloat16 [4, 4096, 1024], P('slab', 'row', 'col')
The draws below stay inside these ranges and needn't reach their ends.
All inputs are finite; a program needn't handle non-finite values.
Results may differ from the reference program's by a relative error of at most 0.008.
Values may be sent and summed in bfloat16 or wider, within the bound.
A program may use at most 128 MiB of HBM per device.

```python
import jax
import jax.numpy as jnp
from jax import lax

M = 4096
SHOTS = 1024
N_SLAB = 4


def block_scale(rng, dims, split, least, largest):
    level = 1.0
    for axis_at, shards_of in split:
        draws = jax.random.uniform(jax.random.fold_in(jax.random.fold_in(rng, 6), axis_at), (shards_of,), jnp.float32, least / len(split), largest / len(split))
        level = level * jnp.repeat(jnp.exp(draws), dims[axis_at] // shards_of).reshape((-1,) + (1,) * (len(dims) - 1 - axis_at))
    return level


def bell_draw(stream_key, extent, spread, limit, split=(), held_as=jnp.bfloat16):
    entries = jax.random.normal(stream_key, extent, jnp.float32) * spread
    if len(split) > 0:
        entries = block_scale(stream_key, extent, split, -0.22, 0.18) * entries
    return jnp.clip(entries, min=-limit, max=limit).astype(held_as)


def setup_inputs(seed: int = 0) -> dict:
    seeds = jax.random.split(jax.random.key(seed), 4)
    reflection = bell_draw(seeds[0], (N_SLAB, M, M), (2 * M) ** -0.5, 0.0625, ((0, 4), (1, 2), (2, 4)))
    transmission = bell_draw(seeds[1], (N_SLAB, M, M), M ** -0.5, 0.09375, ((0, 4), (1, 2), (2, 4)))
    shots = bell_draw(seeds[2], (N_SLAB, M, SHOTS), 1.0, 6.0, ((0, 4), (1, 2), (2, 4)))
    return dict(reflection=reflection, transmission=transmission, shots=shots)


def reference(reflection, transmission, shots):
    results = []
    for slab_index in range(N_SLAB):
        partner = slab_index ^ 1
        first = jnp.dot(transmission[slab_index], shots[slab_index], preferred_element_type=jnp.float32).astype(jnp.bfloat16)
        middle = jnp.dot(reflection[partner].astype(jnp.float32), first.astype(jnp.float32), precision=lax.Precision.HIGHEST)
        bounce = jnp.dot(reflection[slab_index].astype(jnp.float32), middle, precision=lax.Precision.HIGHEST)
        summed = (first.astype(jnp.float32) + bounce).astype(jnp.bfloat16)
        results.append(jnp.dot(transmission[partner], summed, preferred_element_type=jnp.float32).astype(jnp.bfloat16))
    return jnp.stack(results)
```

```python
import jax
import jax.numpy as jnp
from jax import lax
from jax.experimental import pallas as pl
from jax.experimental.pallas import tpu as pltpu
from jax.sharding import PartitionSpec as P

GROUPS = 2


def partner(block, axis, bit):
    count = lax.axis_size(axis)
    route = []
    for low in range(count):
        high = low | 1 << bit
        if high != low and high < count:
            route += [(low, high), (high, low)]
    return lax.ppermute(block, axis, route)


def shift(block, axis, by):
    count = lax.axis_size(axis)
    by %= count
    if by == 0:
        return block
    return lax.ppermute(block, axis, [(i, (i + by) % count) for i in range(count)])


def pick(options, place):
    chosen = options[0]
    for at in range(1, len(options)):
        chosen = jnp.where(place == at, options[at], chosen)
    return chosen


def in_order(relative, me):
    count = len(relative)
    return [pick([relative[(j - at) % count] for at in range(count)], me) for j in range(count)]


def dot(a, b):
    return jnp.dot(a, b, preferred_element_type=jnp.float32)


def on_device(reflection, transmission, shots):
    own_refl = reflection[0]
    own_trans = transmission[0]
    shot_tile = shots[0]
    rows, cols = lax.axis_size("row"), lax.axis_size("col")
    x = lax.axis_index("row")
    bf16 = jnp.bfloat16
    far_refl, far_trans = partner((own_refl, own_trans), "slab", 0)

    width = shot_tile.shape[1] // rows
    kept = []
    for k in range(rows):
        piece = lax.dynamic_slice_in_dim(shot_tile, ((x + k) % rows) * width, width, axis=1)
        kept.append(shift(piece, "row", k))
    face = jnp.concatenate(in_order([kept[-k % rows] for k in range(rows)], x), axis=0)
    depth = face.shape[0] // cols
    face = lax.all_to_all(face.reshape(cols, depth, width), "col", 0, 0)

    groups = GROUPS if cols % GROUPS == 0 else 1
    per = cols // groups
    state = []
    for g in range(groups):
        mine = jnp.concatenate([face[g * per + i] for i in range(per)], axis=1)
        state.append(mine)

    def product(operator, mine):
        pieces = [shift(mine, "row", k) for k in range(rows)]
        sent = [
            shift(dot(operator, pieces[k]).astype(bf16), "row", -k) for k in range(rows)
        ]
        whole = jnp.concatenate(in_order(sent, x), axis=0)
        return lax.psum_scatter(whole, "col", scatter_dimension=0, tiled=True)

    first = [product(own_trans, mine) for mine in state]
    middle = [product(far_refl, mine) for mine in first]
    bounce = [product(own_refl, mine) for mine in middle]
    summed = [
        (a.astype(jnp.float32) + b.astype(jnp.float32)).astype(bf16)
        for a, b in zip(first, bounce)
    ]
    panels = []
    for mine in summed:
        pieces = [shift(mine, "row", k) for k in range(rows)]
        ordered = in_order([pieces[-k % rows] for k in range(rows)], x)
        for i in range(per):
            panels.append(
                jnp.concatenate([o[:, i * width : (i + 1) * width] for o in ordered], axis=1)
            )
    merged = jnp.stack([dot(far_trans, p).astype(bf16) for p in panels])
    merged = lax.psum_scatter(merged, "col", scatter_dimension=0, tiled=True)
    return merged


F32, BF16 = jnp.float32, jnp.bfloat16
ORDER = (0, 3, 1, 2)
LAST = 3
MESH = pl.DeviceIdType.MESH


def chain_kernel(
    refl, trans, shots, out, ops, inbox, faces, kept, stage, parts, far, near, far_last, near_last,
    load_sem, core_send, core_recv, cross_send, cross_recv, init_send, init_recv, face_send, face_recv,
    part_send, part_recv, col_send, far_recv, near_recv,
    last_send, last_far_recv, last_near_recv,
):
    s, x, z = lax.axis_index("slab"), lax.axis_index("row"), lax.axis_index("col")
    other_slab = s + 1 - 2 * (s % 2)
    other_x = 1 - x
    height = trans.shape[0]
    depth = faces.shape[2]
    lanes = faces.shape[3]
    high = z // 2
    end = (z == 0) | (z == 3)
    inner = (z == 1) | (z == 2)

    def blk(k):
        return k + high * (3 - 2 * k)

    def remote(src, dst, send, recv, **where):
        return pltpu.make_async_remote_copy(
            src_ref=src, dst_ref=dst, send_sem=send, recv_sem=recv,
            device_id=where, device_id_type=MESH,
        )

    barrier = pltpu.get_barrier_semaphore()
    pl.semaphore_signal(barrier, inc=1, device_id={"slab": other_slab}, device_id_type=MESH)
    for step in range(1, 8):
        place = (x * 4 + z + step) % 8
        pl.semaphore_signal(
            barrier, inc=1, device_id={"row": place // 4, "col": place % 4}, device_id_type=MESH
        )
    pl.semaphore_wait(barrier, 8)

    loads = [
        pltpu.make_async_copy(trans, ops.at[0], load_sem.at[0]),
        pltpu.make_async_copy(refl, ops.at[2], load_sem.at[1]),
    ]
    for copy in loads:
        copy.start()

    def shot_block(b, c):
        return shots.at[pl.ds(b * depth, depth), pl.ds(pl.multiple_of(c * lanes, lanes), lanes)]

    def cross(b):
        return remote(
            shot_block(b, other_x), inbox.at[b], cross_send.at[b], cross_recv.at[b], row=other_x
        )

    def hand_on(source, b, at, to, act):
        @pl.when(to == z)
        def _():
            if act == "start":
                pltpu.make_async_copy(source, faces.at[z, x], init_recv.at[z]).start()

        @pl.when(to != z)
        def _():
            copy = remote(source, faces.at[z, x], init_send.at[at], init_recv.at[z], col=to)
            copy.start() if act == "start" else copy.wait_send()

    def own_block(b, act):
        hand_on(shot_block(b, x), b, b, 2 * x + b, act)

    def crossed_block(b, act):
        hand_on(inbox.at[b], b, 2 + b, 2 * other_x + b, act)

    for b in range(2):
        cross(b).start()
    for b in range(2):
        own_block(b, "start")

    swaps = [
        remote(refl, ops.at[1], core_send.at[0], core_recv.at[0], slab=other_slab),
        remote(trans, ops.at[3], core_send.at[1], core_recv.at[1], slab=other_slab),
    ]
    for copy in swaps:
        copy.start()
    for b in range(2):
        cross(b).wait_recv()
        crossed_block(b, "start")

    def face_copy(p, g):
        return remote(
            faces.at[g, x], faces.at[g, x], face_send.at[p, g], face_recv.at[p, g], row=other_x
        )

    def face_wait(p, g):
        return remote(
            faces.at[g, other_x], faces.at[g, other_x], face_send.at[p, g], face_recv.at[p, g],
            row=other_x,
        ).wait_recv()

    def half(p, g, which):
        return parts.at[p % 2, g, pl.ds(2 * which, 2)]

    def part_copy(p, g, which):
        return remote(
            stage.at[g], half(p, g, which), part_send.at[p, g], part_recv.at[p, g], row=other_x
        )

    def gather(g):
        pltpu.make_async_copy(faces.at[g, x], faces.at[g, x], init_recv.at[g]).wait()
        face_copy(0, g).start()

    tile = min(depth, 512)
    steps = height // tile
    per = depth // tile

    def multiply(p, g):
        if p == 0 and g == ORDER[0]:
            loads[0].wait()
        if p == 1 and g == ORDER[0]:
            swaps[0].wait_recv()
        if p == 2 and g == ORDER[0]:
            loads[1].wait()
        if p == LAST and g == ORDER[0]:
            swaps[1].wait_recv()
        face_wait(p, g)
        if p < LAST:
            if p > 0:
                part_copy(p - 1, g, x).wait_send()
            both = jnp.concatenate([faces[g, other_x], faces[g, x]], axis=1)
        else:
            both = jnp.concatenate([faces[g, 0], faces[g, 1]], axis=1)

        def body(i, carry):
            rows = pl.multiple_of(i * tile, tile)
            block = i // per
            inside = pl.multiple_of((i % per) * tile, tile)
            value = jnp.dot(
                ops[p, pl.ds(rows, tile), :], both, preferred_element_type=F32
            ).astype(BF16)
            if p < LAST:
                stage[g, block, pl.ds(inside, tile), :] = value[:, :lanes]
                parts[p % 2, g, 2 * x + block, pl.ds(inside, tile), :] = value[:, lanes:]
            else:
                parts[p % 2, g, block, pl.ds(inside, tile), :] = value[:, :lanes]
                parts[p % 2, g, 2 + block, pl.ds(inside, tile), :] = value[:, lanes:]
            return carry

        lax.fori_loop(0, steps, body, 0)
        if p < LAST:
            part_copy(p, g, x).start()

    def block_copy(p, g, k, slot, bank, sems, to, at):
        return remote(
            parts.at[p % 2, g, blk(k)], bank.at[p % 2, g, at],
            col_send.at[p, g, slot], sems.at[p, g, at], col=blk(to),
        )

    def end_copies(p, g):
        return [
            block_copy(p, g, 3, 0, far, far_recv, 1, 0),
            block_copy(p, g, 2, 1, far, far_recv, 1, 1),
            block_copy(p, g, 1, 2, near, near_recv, 1, 0),
        ]

    def inner_copies(p, g):
        return [
            block_copy(p, g, 0, 0, near, near_recv, 0, 0),
            block_copy(p, g, 3, 1, near, near_recv, 3, 1),
            block_copy(p, g, 2, 2, near, near_recv, 2, 1),
        ]

    def last_far(g, b, to):
        return remote(
            parts.at[1, g, b], far_last.at[g, b], last_send.at[g, b, 0], last_far_recv.at[g, b],
            col=to,
        )

    def last_near(g, b, at, to):
        return remote(
            parts.at[1, g, b], near_last.at[at, b], last_send.at[g, b, 1 + at],
            last_near_recv.at[at, b], col=to,
        )

    def is_blk(g, *ks):
        hit = blk(ks[0]) == g
        for k in ks[1:]:
            hit = hit | (blk(k) == g)
        return hit

    def settle(p, g):
        @pl.when(end)
        def _():
            for copy in end_copies(p, g):
                copy.wait_send()

        @pl.when(inner)
        def _():
            for copy in inner_copies(p, g):
                copy.wait_send()

    def begin(p, g):
        if p == LAST:
            @pl.when(end & is_blk(g, 2, 3))
            def _():
                for b in range(4):
                    last_far(g, b, blk(1)).start()

            @pl.when(end & is_blk(g, 1))
            def _():
                for b in range(4):
                    last_near(g, b, 0, blk(1)).start()

            @pl.when(inner & is_blk(g, 0))
            def _():
                for b in range(4):
                    last_near(g, b, 0, blk(0)).start()

            return
        if p > 0:
            settle(p - 1, g)
        remote(
            stage.at[g], half(p, g, other_x), part_send.at[p, g], part_recv.at[p, g], row=other_x
        ).wait_recv()

        @pl.when(end)
        def _():
            for copy in end_copies(p, g):
                copy.start()

        @pl.when(inner)
        def _():
            inner_copies(p, g)[0].start()

    def merge(p, g):
        if p == LAST:
            @pl.when(inner & is_blk(g, 2, 3))
            def _():
                for b in range(4):
                    last_far(g, b, blk(1)).wait_recv()
                    parts[1, g, b] = (
                        parts[1, g, b].astype(F32) + far_last[g, b].astype(F32)
                    ).astype(BF16)
                    last_near(g, b, 1, jnp.int32(g)).start()

            return

        @pl.when(inner)
        def _():
            arrive = end_copies(p, g)
            leave = inner_copies(p, g)
            for at, k in ((0, 3), (1, 2)):
                arrive[at].wait_recv()
                parts[p % 2, g, blk(k)] = (
                    parts[p % 2, g, blk(k)].astype(F32) + far[p % 2, g, at].astype(F32)
                ).astype(BF16)
                leave[1 + at].start()

    def finish(p, g):
        if p == LAST:
            return
        for at in range(2):
            block_copy(p, g, 0, 0, near, near_recv, 0, at).wait_recv()
        total = (
            parts[p % 2, g, z].astype(F32)
            + near[p % 2, g, 0].astype(F32)
            + near[p % 2, g, 1].astype(F32)
        )
        face_copy(p, g).wait_send()
        if p == 0:
            kept[g] = total.astype(BF16)
        if p == 2:
            total = total + kept[g].astype(F32)
        faces[g, x] = total.astype(BF16)
        face_copy(p + 1, g).start()

    order = [(p, g) for p in range(LAST + 1) for g in ORDER]
    for g in ORDER[:2]:
        gather(g)
    multiply(*order[0])
    for g in ORDER[2:]:
        gather(g)
    count = len(order)
    for t in range(count + 2):
        if t < count:
            begin(*order[t])
        if 0 <= t - 1 < count:
            merge(*order[t - 1])
        if t + 1 < count:
            multiply(*order[t + 1])
        if 0 <= t - 2 < count:
            finish(*order[t - 2])

    for g in range(4):
        @pl.when(z == g)
        def _():
            for b in range(4):
                for at in range(2):
                    last_near(g, b, at, z).wait_recv()
                c, h = b // 2, b % 2
                out[pl.ds(h * depth, depth), pl.ds(c * lanes, lanes)] = (
                    parts[1, g, b].astype(F32)
                    + near_last[0, b].astype(F32)
                    + near_last[1, b].astype(F32)
                ).astype(BF16)

    for g in range(4):
        settle(LAST - 1, g)
        face_copy(LAST, g).wait_send()
        part_copy(LAST - 1, g, x).wait_send()

        @pl.when(end & is_blk(g, 2, 3))
        def _():
            for b in range(4):
                last_far(g, b, blk(1)).wait_send()

        @pl.when(end & is_blk(g, 1))
        def _():
            for b in range(4):
                last_near(g, b, 0, blk(1)).wait_send()

        @pl.when(inner & is_blk(g, 0))
        def _():
            for b in range(4):
                last_near(g, b, 0, blk(0)).wait_send()

        @pl.when(inner & is_blk(g, 2, 3))
        def _():
            for b in range(4):
                last_near(g, b, 1, jnp.int32(g)).wait_send()

    for copy in swaps:
        copy.wait_send()
    for b in range(2):
        cross(b).wait_send()
        own_block(b, "wait")
        crossed_block(b, "wait")


def chain(reflection, transmission, shots):
    refl, trans, tile = reflection[0], transmission[0], shots[0]
    height, inner = trans.shape
    lanes = tile.shape[1] // 2
    hbm = pl.BlockSpec(memory_space=pl.ANY)
    dma = pltpu.SemaphoreType.DMA
    block = (inner, lanes)
    out = pl.pallas_call(
        chain_kernel,
        out_shape=jax.ShapeDtypeStruct(tile.shape, BF16),
        in_specs=[hbm] * 3,
        out_specs=pl.BlockSpec(memory_space=pltpu.VMEM),
        scratch_shapes=[
            pltpu.VMEM((4, height, inner), BF16),
            pltpu.VMEM((2,) + block, BF16),
            pltpu.VMEM((4, 2) + block, BF16),
            pltpu.VMEM((4,) + block, BF16),
            pltpu.VMEM((4, 2) + block, BF16),
            pltpu.VMEM((2, 4, 4) + block, BF16),
            pltpu.VMEM((2, 4, 2) + block, BF16),
            pltpu.VMEM((2, 4, 2) + block, BF16),
            pltpu.VMEM((4, 4) + block, BF16),
            pltpu.VMEM((2, 4) + block, BF16),
            dma((2,)), dma((2,)), dma((2,)), dma((2,)), dma((2,)), dma((4,)), dma((4,)),
            dma((4, 4)), dma((4, 4)), dma((3, 4)), dma((3, 4)),
            dma((3, 4, 3)), dma((3, 4, 2)), dma((3, 4, 2)),
            dma((4, 4, 3)), dma((4, 4)), dma((2, 4)),
        ],
        compiler_params=pltpu.CompilerParams(
            collective_id=0, has_side_effects=True, vmem_limit_bytes=60 << 20
        ),
    )(refl, trans, tile)
    return out[None]


def on_slice(reflection, transmission, shots):
    height, inner = transmission.shape[1:]
    fits = (
        lax.axis_size("row") == 2
        and lax.axis_size("col") == 4
        and height == 2 * inner
        and inner % 512 == 0
        and shots.shape[2] % 256 == 0
        and 11 * height * inner < 24 << 20
    )
    if fits:
        return chain(reflection, transmission, shots)
    return on_device(reflection, transmission, shots)


def solution(mesh):
    placed = (P("slab", "row", "col"), P("slab", "row", "col"), P("slab", "row", "col"))
    return jax.shard_map(
        on_slice, mesh=mesh, in_specs=placed, out_specs=P("slab", "row", "col"), check_vma=False
    )
```

```python
import jax
import jax.numpy as jnp
from jax import lax
from jax.experimental import pallas as pl
from jax.experimental.pallas import tpu as pltpu
from jax.sharding import PartitionSpec as P

GROUPS = 2


def partner(block, axis, bit):
    count = lax.axis_size(axis)
    route = []
    for low in range(count):
        high = low | 1 << bit
        if high != low and high < count:
            route += [(low, high), (high, low)]
    return lax.ppermute(block, axis, route)


def shift(block, axis, by):
    count = lax.axis_size(axis)
    by %= count
    if by == 0:
        return block
    return lax.ppermute(block, axis, [(i, (i + by) % count) for i in range(count)])


def pick(options, place):
    chosen = options[0]
    for at in range(1, len(options)):
        chosen = jnp.where(place == at, options[at], chosen)
    return chosen


def in_order(relative, me):
    count = len(relative)
    return [pick([relative[(j - at) % count] for at in range(count)], me) for j in range(count)]


def dot(a, b):
    return jnp.dot(a, b, preferred_element_type=jnp.float32)


def on_device(reflection, transmission, shots):
    own_refl = reflection[0]
    own_trans = transmission[0]
    shot_tile = shots[0]
    rows, cols = lax.axis_size("row"), lax.axis_size("col")
    x = lax.axis_index("row")
    bf16 = jnp.bfloat16
    far_refl, far_trans = partner((own_refl, own_trans), "slab", 0)

    width = shot_tile.shape[1] // rows
    kept = []
    for k in range(rows):
        piece = lax.dynamic_slice_in_dim(shot_tile, ((x + k) % rows) * width, width, axis=1)
        kept.append(shift(piece, "row", k))
    face = jnp.concatenate(in_order([kept[-k % rows] for k in range(rows)], x), axis=0)
    depth = face.shape[0] // cols
    face = lax.all_to_all(face.reshape(cols, depth, width), "col", 0, 0)

    groups = GROUPS if cols % GROUPS == 0 else 1
    per = cols // groups
    state = []
    for g in range(groups):
        mine = jnp.concatenate([face[g * per + i] for i in range(per)], axis=1)
        state.append(mine)

    def product(operator, mine):
        pieces = [shift(mine, "row", k) for k in range(rows)]
        sent = [
            shift(dot(operator, pieces[k]).astype(bf16), "row", -k) for k in range(rows)
        ]
        whole = jnp.concatenate(in_order(sent, x), axis=0)
        return lax.psum_scatter(whole, "col", scatter_dimension=0, tiled=True)

    first = [product(own_trans, mine) for mine in state]
    middle = [product(far_refl, mine) for mine in first]
    bounce = [product(own_refl, mine) for mine in middle]
    summed = [
        (a.astype(jnp.float32) + b.astype(jnp.float32)).astype(bf16)
        for a, b in zip(first, bounce)
    ]
    panels = []
    for mine in summed:
        pieces = [shift(mine, "row", k) for k in range(rows)]
        ordered = in_order([pieces[-k % rows] for k in range(rows)], x)
        for i in range(per):
            panels.append(
                jnp.concatenate([o[:, i * width : (i + 1) * width] for o in ordered], axis=1)
            )
    merged = jnp.stack([dot(far_trans, p).astype(bf16) for p in panels])
    merged = lax.psum_scatter(merged, "col", scatter_dimension=0, tiled=True)
    return merged


F32, BF16 = jnp.float32, jnp.bfloat16
ORDER = (0, 3, 1, 2)
LAST = 3
MESH = pl.DeviceIdType.MESH


def chain_kernel(
    refl, trans, shots, out, ops, inbox, faces, kept, stage, parts, far, near, far_last, near_last,
    load_sem, core_send, core_recv, cross_send, cross_recv, init_send, init_recv, face_send, face_recv,
    part_send, part_recv, col_send, far_recv, near_recv,
    last_send, last_far_recv, last_near_recv,
):
    s, x, z = lax.axis_index("slab"), lax.axis_index("row"), lax.axis_index("col")
    other_slab = s + 1 - 2 * (s % 2)
    other_x = 1 - x
    height = trans.shape[0]
    depth = faces.shape[2]
    lanes = faces.shape[3]
    high = z // 2
    end = (z == 0) | (z == 3)
    inner = (z == 1) | (z == 2)

    def blk(k):
        return k + high * (3 - 2 * k)

    def remote(src, dst, send, recv, **where):
        return pltpu.make_async_remote_copy(
            src_ref=src, dst_ref=dst, send_sem=send, recv_sem=recv,
            device_id=where, device_id_type=MESH,
        )

    barrier = pltpu.get_barrier_semaphore()
    pl.semaphore_signal(barrier, inc=1, device_id={"slab": other_slab}, device_id_type=MESH)
    for step in range(1, 8):
        place = (x * 4 + z + step) % 8
        pl.semaphore_signal(
            barrier, inc=1, device_id={"row": place // 4, "col": place % 4}, device_id_type=MESH
        )
    pl.semaphore_wait(barrier, 8)

    loads = [
        pltpu.make_async_copy(trans, ops.at[0], load_sem.at[0]),
        pltpu.make_async_copy(refl, ops.at[2], load_sem.at[1]),
    ]
    for copy in loads:
        copy.start()

    def shot_block(b, c):
        return shots.at[pl.ds(b * depth, depth), pl.ds(pl.multiple_of(c * lanes, lanes), lanes)]

    def cross(b):
        return remote(
            shot_block(b, other_x), inbox.at[b], cross_send.at[b], cross_recv.at[b], row=other_x
        )

    def hand_on(source, b, at, to, act):
        @pl.when(to == z)
        def _():
            if act == "start":
                pltpu.make_async_copy(source, faces.at[z, x], init_recv.at[z]).start()

        @pl.when(to != z)
        def _():
            copy = remote(source, faces.at[z, x], init_send.at[at], init_recv.at[z], col=to)
            copy.start() if act == "start" else copy.wait_send()

    def own_block(b, act):
        hand_on(shot_block(b, x), b, b, 2 * x + b, act)

    def crossed_block(b, act):
        hand_on(inbox.at[b], b, 2 + b, 2 * other_x + b, act)

    for b in range(2):
        cross(b).start()
    for b in range(2):
        own_block(b, "start")

    swaps = [
        remote(refl, ops.at[1], core_send.at[0], core_recv.at[0], slab=other_slab),
        remote(trans, ops.at[3], core_send.at[1], core_recv.at[1], slab=other_slab),
    ]
    for copy in swaps:
        copy.start()
    for b in range(2):
        cross(b).wait_recv()
        crossed_block(b, "start")

    def face_copy(p, g):
        return remote(
            faces.at[g, x], faces.at[g, x], face_send.at[p, g], face_recv.at[p, g], row=other_x
        )

    def face_wait(p, g):
        return remote(
            faces.at[g, other_x], faces.at[g, other_x], face_send.at[p, g], face_recv.at[p, g],
            row=other_x,
        ).wait_recv()

    def part_copy(p, g, j, which):
        off = turn(j)
        return remote(
            stage.at[g, off], parts.at[p % 2, g, 2 * which + off],
            part_send.at[p, g, j], part_recv.at[p, g, j], row=other_x,
        )

    def turn(j):
        return 1 - high if j == 0 else high

    def gather(g):
        pltpu.make_async_copy(faces.at[g, x], faces.at[g, x], init_recv.at[g]).wait()
        face_copy(0, g).start()

    tile = min(depth, 512)
    per = depth // tile

    def multiply(p, g):
        if p == 0 and g == ORDER[0]:
            loads[0].wait()
        if p == 1 and g == ORDER[0]:
            swaps[0].wait_recv()
        if p == 2 and g == ORDER[0]:
            loads[1].wait()
        if p == LAST and g == ORDER[0]:
            swaps[1].wait_recv()
        face_wait(p, g)
        if p < LAST:
            if p > 0:
                for j in range(2):
                    part_copy(p - 1, g, j, x).wait_send()
                settle(p - 1, g)
            both = jnp.concatenate([faces[g, other_x], faces[g, x]], axis=1)
        else:
            both = jnp.concatenate([faces[g, 0], faces[g, 1]], axis=1)

        def body(i, block):
            inside = pl.multiple_of(i * tile, tile)
            rows = pl.multiple_of(block * depth + inside, tile)
            value = jnp.dot(
                ops[p, pl.ds(rows, tile), :], both, preferred_element_type=F32
            ).astype(BF16)
            if p < LAST:
                stage[g, block, pl.ds(inside, tile), :] = value[:, :lanes]
                parts[p % 2, g, 2 * x + block, pl.ds(inside, tile), :] = value[:, lanes:]
            else:
                parts[p % 2, g, block, pl.ds(inside, tile), :] = value[:, :lanes]
                parts[p % 2, g, 2 + block, pl.ds(inside, tile), :] = value[:, lanes:]
            return block

        for j in range(2):
            lax.fori_loop(0, per, body, turn(j))
            if p < LAST:
                part_copy(p, g, j, x).start()
                send_block(p, g, 2 * x + turn(j))

    def send_block(p, g, block):
        for copy, k in zip(end_copies(p, g), (3, 2, 1)):
            @pl.when(end & (block == blk(k)))
            def _():
                copy.start()

        @pl.when(inner & (block == blk(0)))
        def _():
            inner_copies(p, g)[0].start()

    def block_copy(p, g, k, slot, bank, sems, to, at):
        return remote(
            parts.at[p % 2, g, blk(k)], bank.at[p % 2, g, at],
            col_send.at[p, g, slot], sems.at[p, g, at], col=blk(to),
        )

    def end_copies(p, g):
        return [
            block_copy(p, g, 3, 0, far, far_recv, 1, 0),
            block_copy(p, g, 2, 1, far, far_recv, 1, 1),
            block_copy(p, g, 1, 2, near, near_recv, 1, 0),
        ]

    def inner_copies(p, g):
        return [
            block_copy(p, g, 0, 0, near, near_recv, 0, 0),
            block_copy(p, g, 3, 1, near, near_recv, 3, 1),
            block_copy(p, g, 2, 2, near, near_recv, 2, 1),
        ]

    def last_far(g, b, to):
        return remote(
            parts.at[1, g, b], far_last.at[g, b], last_send.at[g, b, 0], last_far_recv.at[g, b],
            col=to,
        )

    def last_near(g, b, at, to):
        return remote(
            parts.at[1, g, b], near_last.at[at, b], last_send.at[g, b, 1 + at],
            last_near_recv.at[at, b], col=to,
        )

    def is_blk(g, *ks):
        hit = blk(ks[0]) == g
        for k in ks[1:]:
            hit = hit | (blk(k) == g)
        return hit

    def settle(p, g):
        @pl.when(end)
        def _():
            for copy in end_copies(p, g):
                copy.wait_send()

        @pl.when(inner)
        def _():
            for copy in inner_copies(p, g):
                copy.wait_send()

    def begin(p, g):
        if p == LAST:
            @pl.when(end & is_blk(g, 2, 3))
            def _():
                for b in range(4):
                    last_far(g, b, blk(1)).start()

            @pl.when(end & is_blk(g, 1))
            def _():
                for b in range(4):
                    last_near(g, b, 0, blk(1)).start()

            @pl.when(inner & is_blk(g, 0))
            def _():
                for b in range(4):
                    last_near(g, b, 0, blk(0)).start()

            return
        for j in range(2):
            part_copy(p, g, j, other_x).wait_recv()
            send_block(p, g, 2 * other_x + turn(j))

    def merge(p, g):
        if p == LAST:
            @pl.when(inner & is_blk(g, 2, 3))
            def _():
                for b in range(4):
                    last_far(g, b, blk(1)).wait_recv()
                    parts[1, g, b] = (
                        parts[1, g, b].astype(F32) + far_last[g, b].astype(F32)
                    ).astype(BF16)
                    last_near(g, b, 1, jnp.int32(g)).start()

            return

        @pl.when(inner)
        def _():
            arrive = end_copies(p, g)
            leave = inner_copies(p, g)
            for at, k in ((0, 3), (1, 2)):
                arrive[at].wait_recv()
                parts[p % 2, g, blk(k)] = (
                    parts[p % 2, g, blk(k)].astype(F32) + far[p % 2, g, at].astype(F32)
                ).astype(BF16)
                leave[1 + at].start()

    def finish(p, g):
        if p == LAST:
            return
        for at in range(2):
            block_copy(p, g, 0, 0, near, near_recv, 0, at).wait_recv()
        total = (
            parts[p % 2, g, z].astype(F32)
            + near[p % 2, g, 0].astype(F32)
            + near[p % 2, g, 1].astype(F32)
        )
        face_copy(p, g).wait_send()
        if p == 0:
            kept[g] = total.astype(BF16)
        if p == 2:
            total = total + kept[g].astype(F32)
        faces[g, x] = total.astype(BF16)
        face_copy(p + 1, g).start()

    order = [(p, g) for p in range(LAST + 1) for g in ORDER]
    for g in ORDER[:2]:
        gather(g)
    multiply(*order[0])
    for g in ORDER[2:]:
        gather(g)
    count = len(order)
    for t in range(count + 2):
        if t < count:
            begin(*order[t])
        if 0 <= t - 1 < count:
            merge(*order[t - 1])
        if t + 1 < count:
            multiply(*order[t + 1])
        if 0 <= t - 2 < count:
            finish(*order[t - 2])

    for g in range(4):
        @pl.when(z == g)
        def _():
            for b in range(4):
                for at in range(2):
                    last_near(g, b, at, z).wait_recv()
                c, h = b // 2, b % 2
                out[pl.ds(h * depth, depth), pl.ds(c * lanes, lanes)] = (
                    parts[1, g, b].astype(F32)
                    + near_last[0, b].astype(F32)
                    + near_last[1, b].astype(F32)
                ).astype(BF16)

    for g in range(4):
        settle(LAST - 1, g)
        face_copy(LAST, g).wait_send()
        for j in range(2):
            part_copy(LAST - 1, g, j, x).wait_send()

        @pl.when(end & is_blk(g, 2, 3))
        def _():
            for b in range(4):
                last_far(g, b, blk(1)).wait_send()

        @pl.when(end & is_blk(g, 1))
        def _():
            for b in range(4):
                last_near(g, b, 0, blk(1)).wait_send()

        @pl.when(inner & is_blk(g, 0))
        def _():
            for b in range(4):
                last_near(g, b, 0, blk(0)).wait_send()

        @pl.when(inner & is_blk(g, 2, 3))
        def _():
            for b in range(4):
                last_near(g, b, 1, jnp.int32(g)).wait_send()

    for copy in swaps:
        copy.wait_send()
    for b in range(2):
        cross(b).wait_send()
        own_block(b, "wait")
        crossed_block(b, "wait")


def chain(reflection, transmission, shots):
    refl, trans, tile = reflection[0], transmission[0], shots[0]
    height, inner = trans.shape
    lanes = tile.shape[1] // 2
    hbm = pl.BlockSpec(memory_space=pl.ANY)
    dma = pltpu.SemaphoreType.DMA
    block = (inner, lanes)
    out = pl.pallas_call(
        chain_kernel,
        out_shape=jax.ShapeDtypeStruct(tile.shape, BF16),
        in_specs=[hbm] * 3,
        out_specs=pl.BlockSpec(memory_space=pltpu.VMEM),
        scratch_shapes=[
            pltpu.VMEM((4, height, inner), BF16),
            pltpu.VMEM((2,) + block, BF16),
            pltpu.VMEM((4, 2) + block, BF16),
            pltpu.VMEM((4,) + block, BF16),
            pltpu.VMEM((4, 2) + block, BF16),
            pltpu.VMEM((2, 4, 4) + block, BF16),
            pltpu.VMEM((2, 4, 2) + block, BF16),
            pltpu.VMEM((2, 4, 2) + block, BF16),
            pltpu.VMEM((4, 4) + block, BF16),
            pltpu.VMEM((2, 4) + block, BF16),
            dma((2,)), dma((2,)), dma((2,)), dma((2,)), dma((2,)), dma((4,)), dma((4,)),
            dma((4, 4)), dma((4, 4)), dma((3, 4, 2)), dma((3, 4, 2)),
            dma((3, 4, 3)), dma((3, 4, 2)), dma((3, 4, 2)),
            dma((4, 4, 3)), dma((4, 4)), dma((2, 4)),
        ],
        compiler_params=pltpu.CompilerParams(
            collective_id=0, has_side_effects=True, vmem_limit_bytes=60 << 20
        ),
    )(refl, trans, tile)
    return out[None]


def on_slice(reflection, transmission, shots):
    height, inner = transmission.shape[1:]
    fits = (
        lax.axis_size("row") == 2
        and lax.axis_size("col") == 4
        and height == 2 * inner
        and inner % 512 == 0
        and shots.shape[2] % 256 == 0
        and 11 * height * inner < 24 << 20
    )
    if fits:
        return chain(reflection, transmission, shots)
    return on_device(reflection, transmission, shots)


def solution(mesh):
    placed = (P("slab", "row", "col"), P("slab", "row", "col"), P("slab", "row", "col"))
    return jax.shard_map(
        on_slice, mesh=mesh, in_specs=placed, out_specs=P("slab", "row", "col"), check_vma=False
    )
```

```python
import jax
import jax.numpy as jnp
from jax import lax
from jax.experimental import pallas as pl
from jax.experimental.pallas import tpu as pltpu
from jax.sharding import PartitionSpec as P

GROUPS = 2


def partner(block, axis, bit):
    count = lax.axis_size(axis)
    route = []
    for low in range(count):
        high = low | 1 << bit
        if high != low and high < count:
            route += [(low, high), (high, low)]
    return lax.ppermute(block, axis, route)


def shift(block, axis, by):
    count = lax.axis_size(axis)
    by %= count
    if by == 0:
        return block
    return lax.ppermute(block, axis, [(i, (i + by) % count) for i in range(count)])


def pick(options, place):
    chosen = options[0]
    for at in range(1, len(options)):
        chosen = jnp.where(place == at, options[at], chosen)
    return chosen


def in_order(relative, me):
    count = len(relative)
    return [pick([relative[(j - at) % count] for at in range(count)], me) for j in range(count)]


def dot(a, b):
    return jnp.dot(a, b, preferred_element_type=jnp.float32)


def on_device(reflection, transmission, shots):
    own_refl = reflection[0]
    own_trans = transmission[0]
    shot_tile = shots[0]
    rows, cols = lax.axis_size("row"), lax.axis_size("col")
    x = lax.axis_index("row")
    bf16 = jnp.bfloat16
    far_refl, far_trans = partner((own_refl, own_trans), "slab", 0)

    width = shot_tile.shape[1] // rows
    kept = []
    for k in range(rows):
        piece = lax.dynamic_slice_in_dim(shot_tile, ((x + k) % rows) * width, width, axis=1)
        kept.append(shift(piece, "row", k))
    face = jnp.concatenate(in_order([kept[-k % rows] for k in range(rows)], x), axis=0)
    depth = face.shape[0] // cols
    face = lax.all_to_all(face.reshape(cols, depth, width), "col", 0, 0)

    groups = GROUPS if cols % GROUPS == 0 else 1
    per = cols // groups
    state = []
    for g in range(groups):
        mine = jnp.concatenate([face[g * per + i] for i in range(per)], axis=1)
        state.append(mine)

    def product(operator, mine):
        pieces = [shift(mine, "row", k) for k in range(rows)]
        sent = [
            shift(dot(operator, pieces[k]).astype(bf16), "row", -k) for k in range(rows)
        ]
        whole = jnp.concatenate(in_order(sent, x), axis=0)
        return lax.psum_scatter(whole, "col", scatter_dimension=0, tiled=True)

    first = [product(own_trans, mine) for mine in state]
    middle = [product(far_refl, mine) for mine in first]
    bounce = [product(own_refl, mine) for mine in middle]
    summed = [
        (a.astype(jnp.float32) + b.astype(jnp.float32)).astype(bf16)
        for a, b in zip(first, bounce)
    ]
    panels = []
    for mine in summed:
        pieces = [shift(mine, "row", k) for k in range(rows)]
        ordered = in_order([pieces[-k % rows] for k in range(rows)], x)
        for i in range(per):
            panels.append(
                jnp.concatenate([o[:, i * width : (i + 1) * width] for o in ordered], axis=1)
            )
    merged = jnp.stack([dot(far_trans, p).astype(bf16) for p in panels])
    merged = lax.psum_scatter(merged, "col", scatter_dimension=0, tiled=True)
    return merged


F32, BF16 = jnp.float32, jnp.bfloat16
ORDER = (0, 3, 1, 2)
LAST = 3
MESH = pl.DeviceIdType.MESH


def chain_kernel(
    refl, trans, shots, out, ops, inbox, faces, kept, stage, parts, far, near, far_last, near_last,
    load_sem, home_sem, core_send, core_recv, cross_send, cross_recv, init_send, init_recv, face_send, face_recv,
    part_send, part_recv, col_send, far_recv, near_recv,
    last_send, last_far_recv, last_near_recv,
):
    s, x, z = lax.axis_index("slab"), lax.axis_index("row"), lax.axis_index("col")
    other_slab = s + 1 - 2 * (s % 2)
    other_x = 1 - x
    height = trans.shape[0]
    depth = faces.shape[2]
    lanes = faces.shape[3]
    high = z // 2
    end = (z == 0) | (z == 3)
    inner = (z == 1) | (z == 2)
    home = x == high

    def blk(k):
        return k + high * (3 - 2 * k)

    def remote(src, dst, send, recv, **where):
        return pltpu.make_async_remote_copy(
            src_ref=src, dst_ref=dst, send_sem=send, recv_sem=recv,
            device_id=where, device_id_type=MESH,
        )

    barrier = pltpu.get_barrier_semaphore()
    pl.semaphore_signal(barrier, inc=1, device_id={"slab": other_slab}, device_id_type=MESH)
    for step in range(1, 8):
        place = (x * 4 + z + step) % 8
        pl.semaphore_signal(
            barrier, inc=1, device_id={"row": place // 4, "col": place % 4}, device_id_type=MESH
        )
    pl.semaphore_wait(barrier, 8)

    loads = [
        pltpu.make_async_copy(trans, ops.at[0], load_sem.at[0]),
        pltpu.make_async_copy(refl, ops.at[2], load_sem.at[1]),
    ]
    for copy in loads:
        copy.start()

    def shot_block(b, c):
        return shots.at[pl.ds(pl.multiple_of(b * depth, depth), depth), pl.ds(pl.multiple_of(c * lanes, lanes), lanes)]

    def outer(j, at):
        return at if j == 0 else 1 - at

    def cross(j):
        return remote(
            shot_block(outer(j, x), other_x), inbox.at[j], cross_send.at[j], cross_recv.at[j],
            row=other_x,
        )

    def near_home():
        return remote(
            shot_block(z % 2, x), faces.at[z, x], face_send.at[0, z], face_recv.at[0, z],
            row=other_x,
        )

    home_load = pltpu.make_async_copy(
        shot_block(z % 2, other_x), faces.at[z, other_x], home_sem.at[0]
    )

    def hand_on(source, b, at, to, act):
        @pl.when(to == z)
        def _():
            if act == "start":
                pltpu.make_async_copy(source, faces.at[z, x], init_recv.at[z]).start()

        @pl.when(to != z)
        def _():
            copy = remote(source, faces.at[z, x], init_send.at[at], init_recv.at[z], col=to)
            copy.start() if act == "start" else copy.wait_send()

    def own_block(j, act):
        b = outer(j, x)
        hand_on(shot_block(b, x), b, j, 2 * x + b, act)

    def crossed_block(j, act):
        hand_on(inbox.at[j], j, 2 + j, 2 * other_x + outer(j, other_x), act)

    cross(0).start()

    @pl.when(home)
    def _():
        near_home().start()
        home_load.start()

    cross(1).start()
    for j in range(2):
        own_block(j, "start")

    swaps = [
        remote(refl, ops.at[1], core_send.at[0], core_recv.at[0], slab=other_slab),
        remote(trans, ops.at[3], core_send.at[1], core_recv.at[1], slab=other_slab),
    ]
    for copy in swaps:
        copy.start()
    for b in range(2):
        cross(b).wait_recv()
        crossed_block(b, "start")

    def face_copy(p, g):
        return remote(
            faces.at[g, x], faces.at[g, x], face_send.at[p, g], face_recv.at[p, g], row=other_x
        )

    def face_wait(p, g):
        return remote(
            faces.at[g, other_x], faces.at[g, other_x], face_send.at[p, g], face_recv.at[p, g],
            row=other_x,
        ).wait_recv()

    def part_copy(p, g, j, which):
        off = turn(j)
        return remote(
            stage.at[g, off], parts.at[p % 2, g, 2 * which + off],
            part_send.at[p, g, j], part_recv.at[p, g, j], row=other_x,
        )

    def turn(j):
        return 1 - high if j == 0 else high

    def gather(g):
        pltpu.make_async_copy(faces.at[g, x], faces.at[g, x], init_recv.at[g]).wait()

        @pl.when(z != g)
        def _():
            face_copy(0, g).start()

    tile = min(depth, 512)
    per = depth // tile

    def multiply(p, g, opening):
        if opening:
            if p % 2:
                swaps[p // 2].wait_recv()
            else:
                loads[p // 2].wait()
        if p == 0:
            mine = home & (z == g)

            @pl.when(mine)
            def _():
                home_load.wait()

            @pl.when(jnp.logical_not(mine))
            def _():
                face_wait(0, g)
        else:
            face_wait(p, g)
        if p < LAST:
            if p > 0:
                for j in range(2):
                    part_copy(p - 1, g, j, x).wait_send()
                settle(p - 1, g)
            both = jnp.concatenate([faces[g, other_x], faces[g, x]], axis=1)
        else:
            both = jnp.concatenate([faces[g, 0], faces[g, 1]], axis=1)

        def body(i, block):
            inside = pl.multiple_of(i * tile, tile)
            rows = pl.multiple_of(block * depth + inside, tile)
            value = jnp.dot(
                ops[p, pl.ds(rows, tile), :], both, preferred_element_type=F32
            ).astype(BF16)
            if p < LAST:
                stage[g, block, pl.ds(inside, tile), :] = value[:, :lanes]
                parts[p % 2, g, 2 * x + block, pl.ds(inside, tile), :] = value[:, lanes:]
            else:
                parts[p % 2, g, block, pl.ds(inside, tile), :] = value[:, :lanes]
                parts[p % 2, g, 2 + block, pl.ds(inside, tile), :] = value[:, lanes:]
            return block

        for j in range(2):
            lax.fori_loop(0, per, body, turn(j))
            if p < LAST:
                part_copy(p, g, j, x).start()
                send_block(p, g, 2 * x + turn(j))

    def send_block(p, g, block):
        for copy, k in zip(end_copies(p, g), (3, 2, 1)):
            @pl.when(end & (block == blk(k)))
            def _():
                copy.start()

        @pl.when(inner & (block == blk(0)))
        def _():
            inner_copies(p, g)[0].start()

    def block_copy(p, g, k, slot, bank, sems, to, at):
        return remote(
            parts.at[p % 2, g, blk(k)], bank.at[p % 2, g, at],
            col_send.at[p, g, slot], sems.at[p, g, at], col=blk(to),
        )

    def end_copies(p, g):
        return [
            block_copy(p, g, 3, 0, far, far_recv, 1, 0),
            block_copy(p, g, 2, 1, far, far_recv, 1, 1),
            block_copy(p, g, 1, 2, near, near_recv, 1, 0),
        ]

    def inner_copies(p, g):
        return [
            block_copy(p, g, 0, 0, near, near_recv, 0, 0),
            block_copy(p, g, 3, 1, near, near_recv, 3, 1),
            block_copy(p, g, 2, 2, near, near_recv, 2, 1),
        ]

    def last_far(g, b, to):
        return remote(
            parts.at[1, g, b], far_last.at[g, b], last_send.at[g, b, 0], last_far_recv.at[g, b],
            col=to,
        )

    def last_near(g, b, at, to):
        return remote(
            parts.at[1, g, b], near_last.at[at, b], last_send.at[g, b, 1 + at],
            last_near_recv.at[at, b], col=to,
        )

    def is_blk(g, *ks):
        hit = blk(ks[0]) == g
        for k in ks[1:]:
            hit = hit | (blk(k) == g)
        return hit

    def settle(p, g):
        @pl.when(end)
        def _():
            for copy in end_copies(p, g):
                copy.wait_send()

        @pl.when(inner)
        def _():
            for copy in inner_copies(p, g):
                copy.wait_send()

    def begin(p, g):
        if p == LAST:
            @pl.when(end & is_blk(g, 2, 3))
            def _():
                for b in range(4):
                    last_far(g, b, blk(1)).start()

            @pl.when(end & is_blk(g, 1))
            def _():
                for b in range(4):
                    last_near(g, b, 0, blk(1)).start()

            @pl.when(inner & is_blk(g, 0))
            def _():
                for b in range(4):
                    last_near(g, b, 0, blk(0)).start()

            return
        for j in range(2):
            part_copy(p, g, j, other_x).wait_recv()
            send_block(p, g, 2 * other_x + turn(j))

    def merge(p, g):
        if p == LAST:
            @pl.when(inner & is_blk(g, 2, 3))
            def _():
                for b in range(4):
                    last_far(g, b, blk(1)).wait_recv()
                    parts[1, g, b] = (
                        parts[1, g, b].astype(F32) + far_last[g, b].astype(F32)
                    ).astype(BF16)
                    last_near(g, b, 1, g).start()

            return

        @pl.when(inner)
        def _():
            arrive = end_copies(p, g)
            leave = inner_copies(p, g)
            for at, k in ((0, 3), (1, 2)):
                arrive[at].wait_recv()
                parts[p % 2, g, blk(k)] = (
                    parts[p % 2, g, blk(k)].astype(F32) + far[p % 2, g, at].astype(F32)
                ).astype(BF16)
                leave[1 + at].start()

    def finish(p, g):
        if p == LAST:
            return
        for at in range(2):
            block_copy(p, g, 0, 0, near, near_recv, 0, at).wait_recv()
        total = (
            parts[p % 2, g, z].astype(F32)
            + near[p % 2, g, 0].astype(F32)
            + near[p % 2, g, 1].astype(F32)
        )
        if p == 0:
            @pl.when(home | (z != g))
            def _():
                face_copy(p, g).wait_send()
        else:
            face_copy(p, g).wait_send()
        if p == 0:
            kept[g] = total.astype(BF16)
        if p == 2:
            total = total + kept[g].astype(F32)
        faces[g, x] = total.astype(BF16)
        face_copy(p + 1, g).start()

    order = [(0, blk(g)) for g in ORDER]
    order += [(p, g) for p in range(1, LAST) for g in ORDER]
    order += [(LAST, blk(g)) for g in (0, 3, 2, 1)]
    count = len(order)

    def advance(t):
        multiply(*order[t], opening=t % 4 == 0)

    gather(order[0][1])
    advance(0)
    for t in range(1, 4):
        gather(order[t][1])
    for t in range(count + 2):
        if 0 <= t - 1 < count:
            merge(*order[t - 1])
        if t in (2, 4):
            for g in ORDER[t - 2 : t]:
                finish(0, g)
        if 4 <= t - 2 < count:
            finish(*order[t - 2])
        if t < count:
            begin(*order[t])
        if t + 1 < count:
            advance(t + 1)

    for g in range(4):
        @pl.when(z == g)
        def _():
            for b in range(4):
                for at in range(2):
                    last_near(g, b, at, z).wait_recv()
                c, h = b // 2, b % 2
                out[pl.ds(h * depth, depth), pl.ds(c * lanes, lanes)] = (
                    parts[1, g, b].astype(F32)
                    + near_last[0, b].astype(F32)
                    + near_last[1, b].astype(F32)
                ).astype(BF16)

    for g in range(4):
        settle(LAST - 1, g)
        face_copy(LAST, g).wait_send()
        for j in range(2):
            part_copy(LAST - 1, g, j, x).wait_send()

        @pl.when(end & is_blk(g, 2, 3))
        def _():
            for b in range(4):
                last_far(g, b, blk(1)).wait_send()

        @pl.when(end & is_blk(g, 1))
        def _():
            for b in range(4):
                last_near(g, b, 0, blk(1)).wait_send()

        @pl.when(inner & is_blk(g, 0))
        def _():
            for b in range(4):
                last_near(g, b, 0, blk(0)).wait_send()

        @pl.when(inner & is_blk(g, 2, 3))
        def _():
            for b in range(4):
                last_near(g, b, 1, jnp.int32(g)).wait_send()

    for copy in swaps:
        copy.wait_send()
    for b in range(2):
        cross(b).wait_send()
        own_block(b, "wait")
        crossed_block(b, "wait")


def chain(reflection, transmission, shots):
    refl, trans, tile = reflection[0], transmission[0], shots[0]
    height, inner = trans.shape
    lanes = tile.shape[1] // 2
    hbm = pl.BlockSpec(memory_space=pl.ANY)
    dma = pltpu.SemaphoreType.DMA
    block = (inner, lanes)
    out = pl.pallas_call(
        chain_kernel,
        out_shape=jax.ShapeDtypeStruct(tile.shape, BF16),
        in_specs=[hbm] * 3,
        out_specs=pl.BlockSpec(memory_space=pltpu.VMEM),
        scratch_shapes=[
            pltpu.VMEM((4, height, inner), BF16),
            pltpu.VMEM((2,) + block, BF16),
            pltpu.VMEM((4, 2) + block, BF16),
            pltpu.VMEM((4,) + block, BF16),
            pltpu.VMEM((4, 2) + block, BF16),
            pltpu.VMEM((2, 4, 4) + block, BF16),
            pltpu.VMEM((2, 4, 2) + block, BF16),
            pltpu.VMEM((2, 4, 2) + block, BF16),
            pltpu.VMEM((4, 4) + block, BF16),
            pltpu.VMEM((2, 4) + block, BF16),
            dma((2,)), dma((1,)), dma((2,)), dma((2,)), dma((2,)), dma((2,)), dma((4,)), dma((4,)),
            dma((4, 4)), dma((4, 4)), dma((3, 4, 2)), dma((3, 4, 2)),
            dma((3, 4, 3)), dma((3, 4, 2)), dma((3, 4, 2)),
            dma((4, 4, 3)), dma((4, 4)), dma((2, 4)),
        ],
        compiler_params=pltpu.CompilerParams(
            collective_id=0, has_side_effects=True, vmem_limit_bytes=60 << 20
        ),
    )(refl, trans, tile)
    return out[None]


def on_slice(reflection, transmission, shots):
    height, inner = transmission.shape[1:]
    fits = (
        lax.axis_size("row") == 2
        and lax.axis_size("col") == 4
        and height == 2 * inner
        and inner % 512 == 0
        and shots.shape[2] % 256 == 0
        and 11 * height * inner < 24 << 20
    )
    if fits:
        return chain(reflection, transmission, shots)
    return on_device(reflection, transmission, shots)


def solution(mesh):
    placed = (P("slab", "row", "col"), P("slab", "row", "col"), P("slab", "row", "col"))
    return jax.shard_map(
        on_slice, mesh=mesh, in_specs=placed, out_specs=P("slab", "row", "col"), check_vma=False
    )
```

```python
import jax
import jax.numpy as jnp
from jax import lax
from jax.experimental import pallas as pl
from jax.experimental.pallas import tpu as pltpu
from jax.sharding import PartitionSpec as P

GROUPS = 2


def partner(block, axis, bit):
    count = lax.axis_size(axis)
    route = []
    for low in range(count):
        high = low | 1 << bit
        if high != low and high < count:
            route += [(low, high), (high, low)]
    return lax.ppermute(block, axis, route)


def shift(block, axis, by):
    count = lax.axis_size(axis)
    by %= count
    if by == 0:
        return block
    return lax.ppermute(block, axis, [(i, (i + by) % count) for i in range(count)])


def pick(options, place):
    chosen = options[0]
    for at in range(1, len(options)):
        chosen = jnp.where(place == at, options[at], chosen)
    return chosen


def in_order(relative, me):
    count = len(relative)
    return [pick([relative[(j - at) % count] for at in range(count)], me) for j in range(count)]


def dot(a, b):
    return jnp.dot(a, b, preferred_element_type=jnp.float32)


def on_device(reflection, transmission, shots):
    own_refl = reflection[0]
    own_trans = transmission[0]
    shot_tile = shots[0]
    rows, cols = lax.axis_size("row"), lax.axis_size("col")
    x = lax.axis_index("row")
    bf16 = jnp.bfloat16
    far_refl, far_trans = partner((own_refl, own_trans), "slab", 0)

    width = shot_tile.shape[1] // rows
    kept = []
    for k in range(rows):
        piece = lax.dynamic_slice_in_dim(shot_tile, ((x + k) % rows) * width, width, axis=1)
        kept.append(shift(piece, "row", k))
    face = jnp.concatenate(in_order([kept[-k % rows] for k in range(rows)], x), axis=0)
    depth = face.shape[0] // cols
    face = lax.all_to_all(face.reshape(cols, depth, width), "col", 0, 0)

    groups = GROUPS if cols % GROUPS == 0 else 1
    per = cols // groups
    state = []
    for g in range(groups):
        mine = jnp.concatenate([face[g * per + i] for i in range(per)], axis=1)
        state.append(mine)

    def product(operator, mine):
        pieces = [shift(mine, "row", k) for k in range(rows)]
        sent = [
            shift(dot(operator, pieces[k]).astype(bf16), "row", -k) for k in range(rows)
        ]
        whole = jnp.concatenate(in_order(sent, x), axis=0)
        return lax.psum_scatter(whole, "col", scatter_dimension=0, tiled=True)

    first = [product(own_trans, mine) for mine in state]
    middle = [product(far_refl, mine) for mine in first]
    bounce = [product(own_refl, mine) for mine in middle]
    summed = [
        (a.astype(jnp.float32) + b.astype(jnp.float32)).astype(bf16)
        for a, b in zip(first, bounce)
    ]
    panels = []
    for mine in summed:
        pieces = [shift(mine, "row", k) for k in range(rows)]
        ordered = in_order([pieces[-k % rows] for k in range(rows)], x)
        for i in range(per):
            panels.append(
                jnp.concatenate([o[:, i * width : (i + 1) * width] for o in ordered], axis=1)
            )
    merged = jnp.stack([dot(far_trans, p).astype(bf16) for p in panels])
    merged = lax.psum_scatter(merged, "col", scatter_dimension=0, tiled=True)
    return merged


F32, BF16 = jnp.float32, jnp.bfloat16
ORDER = (0, 3, 1, 2)
LAST = 3
MESH = pl.DeviceIdType.MESH


def chain_kernel(
    refl, trans, shots, out, ops, inbox, faces, kept, stage, parts, far, near, far_last, near_last,
    load_sem, home_sem, core_send, core_recv, cross_send, cross_recv, init_send, init_recv, face_send, face_recv,
    part_send, part_recv, col_send, far_recv, near_recv,
    last_send, last_far_recv, last_near_recv,
):
    s, x, z = lax.axis_index("slab"), lax.axis_index("row"), lax.axis_index("col")
    other_slab = s + 1 - 2 * (s % 2)
    other_x = 1 - x
    height = trans.shape[0]
    depth = faces.shape[2]
    lanes = faces.shape[3]
    high = z // 2
    end = (z == 0) | (z == 3)
    inner = (z == 1) | (z == 2)
    home = x == high

    def blk(k):
        return k + high * (3 - 2 * k)

    def remote(src, dst, send, recv, **where):
        return pltpu.make_async_remote_copy(
            src_ref=src, dst_ref=dst, send_sem=send, recv_sem=recv,
            device_id=where, device_id_type=MESH,
        )

    barrier = pltpu.get_barrier_semaphore()
    pl.semaphore_signal(barrier, inc=1, device_id={"slab": other_slab}, device_id_type=MESH)
    for step in range(1, 8):
        place = (x * 4 + z + step) % 8
        pl.semaphore_signal(
            barrier, inc=1, device_id={"row": place // 4, "col": place % 4}, device_id_type=MESH
        )
    pl.semaphore_wait(barrier, 8)

    loads = [
        pltpu.make_async_copy(trans, ops.at[0], load_sem.at[0]),
        pltpu.make_async_copy(refl, ops.at[2], load_sem.at[1]),
    ]
    for copy in loads:
        copy.start()

    def shot_block(b, c):
        return shots.at[pl.ds(pl.multiple_of(b * depth, depth), depth), pl.ds(pl.multiple_of(c * lanes, lanes), lanes)]

    def outer(j, at):
        return at if j == 0 else 1 - at

    def cross(j):
        return remote(
            shot_block(outer(j, x), other_x), inbox.at[j], cross_send.at[j], cross_recv.at[j],
            row=other_x,
        )

    def near_home():
        return remote(
            shot_block(z % 2, x), faces.at[z, x], face_send.at[0, z], face_recv.at[0, z],
            row=other_x,
        )

    home_load = pltpu.make_async_copy(
        shot_block(z % 2, other_x), faces.at[z, other_x], home_sem.at[0]
    )

    def hand_on(source, b, at, to, act):
        @pl.when(to == z)
        def _():
            if act == "start":
                pltpu.make_async_copy(source, faces.at[z, x], init_recv.at[z]).start()

        @pl.when(to != z)
        def _():
            copy = remote(source, faces.at[z, x], init_send.at[at], init_recv.at[z], col=to)
            copy.start() if act == "start" else copy.wait_send()

    def own_block(j, act):
        b = outer(j, x)
        hand_on(shot_block(b, x), b, j, 2 * x + b, act)

    def crossed_block(j, act):
        hand_on(inbox.at[j], j, 2 + j, 2 * other_x + outer(j, other_x), act)

    cross(0).start()

    @pl.when(home)
    def _():
        near_home().start()
        home_load.start()

    cross(1).start()
    for j in range(2):
        own_block(j, "start")

    swaps = [
        remote(refl, ops.at[1], core_send.at[0], core_recv.at[0], slab=other_slab),
        remote(trans, ops.at[3], core_send.at[1], core_recv.at[1], slab=other_slab),
    ]
    for copy in swaps:
        copy.start()
    for b in range(2):
        cross(b).wait_recv()
        crossed_block(b, "start")

    def face_copy(p, g):
        return remote(
            faces.at[g, x], faces.at[g, x], face_send.at[p, g], face_recv.at[p, g], row=other_x
        )

    def face_wait(p, g):
        return remote(
            faces.at[g, other_x], faces.at[g, other_x], face_send.at[p, g], face_recv.at[p, g],
            row=other_x,
        ).wait_recv()

    def part_copy(p, g, j, which):
        off = turn(j)
        return remote(
            stage.at[g, off], parts.at[p % 2, g, 2 * which + off],
            part_send.at[p, g, j], part_recv.at[p, g, j], row=other_x,
        )

    def turn(j):
        return 1 - high if j == 0 else high

    def gather(g):
        pltpu.make_async_copy(faces.at[g, x], faces.at[g, x], init_recv.at[g]).wait()

        @pl.when(z != g)
        def _():
            face_copy(0, g).start()

    tile = min(depth, 512)
    per = depth // tile

    def multiply(p, g, opening):
        if opening:
            if p % 2:
                swaps[p // 2].wait_recv()
            else:
                loads[p // 2].wait()
        if p == 0:
            mine = home & (z == g)

            @pl.when(mine)
            def _():
                home_load.wait()

            @pl.when(jnp.logical_not(mine))
            def _():
                face_wait(0, g)
        else:
            face_wait(p, g)
        if p < LAST:
            if p > 0:
                for j in range(2):
                    part_copy(p - 1, g, j, x).wait_send()
                settle(p - 1, g)
            both = jnp.concatenate([faces[g, other_x], faces[g, x]], axis=1)
        else:
            both = jnp.concatenate([faces[g, 0], faces[g, 1]], axis=1)

        def body(i, block):
            inside = pl.multiple_of(i * tile, tile)
            rows = pl.multiple_of(block * depth + inside, tile)
            value = jnp.dot(
                ops[p, pl.ds(rows, tile), :], both, preferred_element_type=F32
            ).astype(BF16)
            if p < LAST:
                stage[g, block, pl.ds(inside, tile), :] = value[:, :lanes]
                parts[p % 2, g, 2 * x + block, pl.ds(inside, tile), :] = value[:, lanes:]
            else:
                parts[p % 2, g, block, pl.ds(inside, tile), :] = value[:, :lanes]
                parts[p % 2, g, 2 + block, pl.ds(inside, tile), :] = value[:, lanes:]
            return block

        for j in range(2):
            lax.fori_loop(0, per, body, turn(j) if p < LAST else j)
            if p < LAST:
                part_copy(p, g, j, x).start()
                send_block(p, g, 2 * x + turn(j))
            else:
                send_last(g, (j, 2 + j))

    def send_last(g, blocks):
        @pl.when(end & is_blk(g, 2, 3))
        def _():
            for b in blocks:
                last_far(g, b, blk(1)).start()

        @pl.when(end & is_blk(g, 1))
        def _():
            for b in blocks:
                last_near(g, b, 0, blk(1)).start()

        @pl.when(inner & is_blk(g, 0))
        def _():
            for b in blocks:
                last_near(g, b, 0, blk(0)).start()

    def send_block(p, g, block):
        for copy, k in zip(end_copies(p, g), (3, 2, 1)):
            @pl.when(end & (block == blk(k)))
            def _():
                copy.start()

        @pl.when(inner & (block == blk(0)))
        def _():
            inner_copies(p, g)[0].start()

    def block_copy(p, g, k, slot, bank, sems, to, at):
        return remote(
            parts.at[p % 2, g, blk(k)], bank.at[p % 2, g, at],
            col_send.at[p, g, slot], sems.at[p, g, at], col=blk(to),
        )

    def end_copies(p, g):
        return [
            block_copy(p, g, 3, 0, far, far_recv, 1, 0),
            block_copy(p, g, 2, 1, far, far_recv, 1, 1),
            block_copy(p, g, 1, 2, near, near_recv, 1, 0),
        ]

    def inner_copies(p, g):
        return [
            block_copy(p, g, 0, 0, near, near_recv, 0, 0),
            block_copy(p, g, 3, 1, near, near_recv, 3, 1),
            block_copy(p, g, 2, 2, near, near_recv, 2, 1),
        ]

    def last_far(g, b, to):
        return remote(
            parts.at[1, g, b], far_last.at[g, b], last_send.at[g, b, 0], last_far_recv.at[g, b],
            col=to,
        )

    def last_near(g, b, at, to):
        return remote(
            parts.at[1, g, b], near_last.at[at, b], last_send.at[g, b, 1 + at],
            last_near_recv.at[at, b], col=to,
        )

    def is_blk(g, *ks):
        hit = blk(ks[0]) == g
        for k in ks[1:]:
            hit = hit | (blk(k) == g)
        return hit

    def settle(p, g):
        @pl.when(end)
        def _():
            for copy in end_copies(p, g):
                copy.wait_send()

        @pl.when(inner)
        def _():
            for copy in inner_copies(p, g):
                copy.wait_send()

    def begin(p, g):
        if p == LAST:
            return
        for j in range(2):
            part_copy(p, g, j, other_x).wait_recv()
            send_block(p, g, 2 * other_x + turn(j))

    def merge(p, g):
        if p == LAST:
            @pl.when(inner & is_blk(g, 2, 3))
            def _():
                for b in (0, 2, 1, 3):
                    last_far(g, b, blk(1)).wait_recv()
                    parts[1, g, b] = (
                        parts[1, g, b].astype(F32) + far_last[g, b].astype(F32)
                    ).astype(BF16)
                    last_near(g, b, 1, g).start()

            return

        @pl.when(inner)
        def _():
            arrive = end_copies(p, g)
            leave = inner_copies(p, g)
            for at, k in ((0, 3), (1, 2)):
                arrive[at].wait_recv()
                parts[p % 2, g, blk(k)] = (
                    parts[p % 2, g, blk(k)].astype(F32) + far[p % 2, g, at].astype(F32)
                ).astype(BF16)
                leave[1 + at].start()

    def finish(p, g):
        if p == LAST:
            return
        for at in range(2):
            block_copy(p, g, 0, 0, near, near_recv, 0, at).wait_recv()
        total = (
            parts[p % 2, g, z].astype(F32)
            + near[p % 2, g, 0].astype(F32)
            + near[p % 2, g, 1].astype(F32)
        )
        if p == 0:
            @pl.when(home | (z != g))
            def _():
                face_copy(p, g).wait_send()
        else:
            face_copy(p, g).wait_send()
        if p == 0:
            kept[g] = total.astype(BF16)
        if p == 2:
            total = total + kept[g].astype(F32)
        faces[g, x] = total.astype(BF16)
        face_copy(p + 1, g).start()

    order = [(0, blk(g)) for g in ORDER]
    order += [(p, g) for p in range(1, LAST) for g in ORDER]
    order += [(LAST, blk(g)) for g in (3, 0, 2, 1)]
    count = len(order)

    def advance(t):
        multiply(*order[t], opening=t % 4 == 0)

    gather(order[0][1])
    advance(0)
    for t in range(1, 4):
        gather(order[t][1])
    for t in range(count + 2):
        if t in (3, 5):
            for g in ORDER[t - 3 : t - 1]:
                finish(0, g)
        if 4 <= t - 2 < count:
            finish(*order[t - 2])
        if 0 <= t - 1 < count:
            merge(*order[t - 1])
        if t < count:
            begin(*order[t])
        if t + 1 < count:
            advance(t + 1)

    for g in range(4):
        @pl.when(z == g)
        def _():
            for b in (0, 2, 1, 3):
                for at in range(2):
                    last_near(g, b, at, z).wait_recv()
                c, h = b // 2, b % 2
                out[pl.ds(h * depth, depth), pl.ds(c * lanes, lanes)] = (
                    parts[1, g, b].astype(F32)
                    + near_last[0, b].astype(F32)
                    + near_last[1, b].astype(F32)
                ).astype(BF16)

    for g in range(4):
        settle(LAST - 1, g)
        face_copy(LAST, g).wait_send()
        for j in range(2):
            part_copy(LAST - 1, g, j, x).wait_send()

        @pl.when(end & is_blk(g, 2, 3))
        def _():
            for b in range(4):
                last_far(g, b, blk(1)).wait_send()

        @pl.when(end & is_blk(g, 1))
        def _():
            for b in range(4):
                last_near(g, b, 0, blk(1)).wait_send()

        @pl.when(inner & is_blk(g, 0))
        def _():
            for b in range(4):
                last_near(g, b, 0, blk(0)).wait_send()

        @pl.when(inner & is_blk(g, 2, 3))
        def _():
            for b in range(4):
                last_near(g, b, 1, jnp.int32(g)).wait_send()

    for copy in swaps:
        copy.wait_send()
    for b in range(2):
        cross(b).wait_send()
        own_block(b, "wait")
        crossed_block(b, "wait")


def chain(reflection, transmission, shots):
    refl, trans, tile = reflection[0], transmission[0], shots[0]
    height, inner = trans.shape
    lanes = tile.shape[1] // 2
    hbm = pl.BlockSpec(memory_space=pl.ANY)
    dma = pltpu.SemaphoreType.DMA
    block = (inner, lanes)
    out = pl.pallas_call(
        chain_kernel,
        out_shape=jax.ShapeDtypeStruct(tile.shape, BF16),
        in_specs=[hbm] * 3,
        out_specs=pl.BlockSpec(memory_space=pltpu.VMEM),
        scratch_shapes=[
            pltpu.VMEM((4, height, inner), BF16),
            pltpu.VMEM((2,) + block, BF16),
            pltpu.VMEM((4, 2) + block, BF16),
            pltpu.VMEM((4,) + block, BF16),
            pltpu.VMEM((4, 2) + block, BF16),
            pltpu.VMEM((2, 4, 4) + block, BF16),
            pltpu.VMEM((2, 4, 2) + block, BF16),
            pltpu.VMEM((2, 4, 2) + block, BF16),
            pltpu.VMEM((4, 4) + block, BF16),
            pltpu.VMEM((2, 4) + block, BF16),
            dma((2,)), dma((1,)), dma((2,)), dma((2,)), dma((2,)), dma((2,)), dma((4,)), dma((4,)),
            dma((4, 4)), dma((4, 4)), dma((3, 4, 2)), dma((3, 4, 2)),
            dma((3, 4, 3)), dma((3, 4, 2)), dma((3, 4, 2)),
            dma((4, 4, 3)), dma((4, 4)), dma((2, 4)),
        ],
        compiler_params=pltpu.CompilerParams(
            collective_id=0, has_side_effects=True, vmem_limit_bytes=60 << 20
        ),
    )(refl, trans, tile)
    return out[None]


def on_slice(reflection, transmission, shots):
    height, inner = transmission.shape[1:]
    fits = (
        lax.axis_size("row") == 2
        and lax.axis_size("col") == 4
        and height == 2 * inner
        and inner % 512 == 0
        and shots.shape[2] % 256 == 0
        and 11 * height * inner < 24 << 20
    )
    if fits:
        return chain(reflection, transmission, shots)
    return on_device(reflection, transmission, shots)


def solution(mesh):
    placed = (P("slab", "row", "col"), P("slab", "row", "col"), P("slab", "row", "col"))
    return jax.shard_map(
        on_slice, mesh=mesh, in_specs=placed, out_specs=P("slab", "row", "col"), check_vma=False
    )
```

```python
import jax
import jax.numpy as jnp
from jax import lax
from jax.experimental import pallas as pl
from jax.experimental.pallas import tpu as pltpu
from jax.sharding import PartitionSpec as P

GROUPS = 2


def partner(block, axis, bit):
    count = lax.axis_size(axis)
    route = []
    for low in range(count):
        high = low | 1 << bit
        if high != low and high < count:
            route += [(low, high), (high, low)]
    return lax.ppermute(block, axis, route)


def shift(block, axis, by):
    count = lax.axis_size(axis)
    by %= count
    if by == 0:
        return block
    return lax.ppermute(block, axis, [(i, (i + by) % count) for i in range(count)])


def pick(options, place):
    chosen = options[0]
    for at in range(1, len(options)):
        chosen = jnp.where(place == at, options[at], chosen)
    return chosen


def in_order(relative, me):
    count = len(relative)
    return [pick([relative[(j - at) % count] for at in range(count)], me) for j in range(count)]


def dot(a, b):
    return jnp.dot(a, b, preferred_element_type=jnp.float32)


def on_device(reflection, transmission, shots):
    own_refl = reflection[0]
    own_trans = transmission[0]
    shot_tile = shots[0]
    rows, cols = lax.axis_size("row"), lax.axis_size("col")
    x = lax.axis_index("row")
    bf16 = jnp.bfloat16
    far_refl, far_trans = partner((own_refl, own_trans), "slab", 0)

    width = shot_tile.shape[1] // rows
    kept = []
    for k in range(rows):
        piece = lax.dynamic_slice_in_dim(shot_tile, ((x + k) % rows) * width, width, axis=1)
        kept.append(shift(piece, "row", k))
    face = jnp.concatenate(in_order([kept[-k % rows] for k in range(rows)], x), axis=0)
    depth = face.shape[0] // cols
    face = lax.all_to_all(face.reshape(cols, depth, width), "col", 0, 0)

    groups = GROUPS if cols % GROUPS == 0 else 1
    per = cols // groups
    state = []
    for g in range(groups):
        mine = jnp.concatenate([face[g * per + i] for i in range(per)], axis=1)
        state.append(mine)

    def product(operator, mine):
        pieces = [shift(mine, "row", k) for k in range(rows)]
        sent = [
            shift(dot(operator, pieces[k]).astype(bf16), "row", -k) for k in range(rows)
        ]
        whole = jnp.concatenate(in_order(sent, x), axis=0)
        return lax.psum_scatter(whole, "col", scatter_dimension=0, tiled=True)

    first = [product(own_trans, mine) for mine in state]
    middle = [product(far_refl, mine) for mine in first]
    bounce = [product(own_refl, mine) for mine in middle]
    summed = [
        (a.astype(jnp.float32) + b.astype(jnp.float32)).astype(bf16)
        for a, b in zip(first, bounce)
    ]
    panels = []
    for mine in summed:
        pieces = [shift(mine, "row", k) for k in range(rows)]
        ordered = in_order([pieces[-k % rows] for k in range(rows)], x)
        for i in range(per):
            panels.append(
                jnp.concatenate([o[:, i * width : (i + 1) * width] for o in ordered], axis=1)
            )
    merged = jnp.stack([dot(far_trans, p).astype(bf16) for p in panels])
    merged = lax.psum_scatter(merged, "col", scatter_dimension=0, tiled=True)
    return merged


F32, BF16 = jnp.float32, jnp.bfloat16
ORDER = (0, 3, 1, 2)
LAST = 3
MESH = pl.DeviceIdType.MESH


def chain_kernel(
    refl, trans, shots, out, total_out, ops, inbox, faces, kept, stage, parts, far, near, far_last, near_last,
    load_sem, home_sem, core_send, core_recv, cross_send, cross_recv, init_send, init_recv, face_send, face_recv,
    part_send, part_recv, col_send, far_recv, near_recv,
    last_send, last_far_recv, last_near_recv, out_sem,
):
    s, x, z = lax.axis_index("slab"), lax.axis_index("row"), lax.axis_index("col")
    other_slab = s + 1 - 2 * (s % 2)
    other_x = 1 - x
    height = trans.shape[0]
    depth = faces.shape[2]
    lanes = faces.shape[3]
    high = z // 2
    end = (z == 0) | (z == 3)
    inner = (z == 1) | (z == 2)
    home = x == high

    def blk(k):
        return k + high * (3 - 2 * k)

    def remote(src, dst, send, recv, **where):
        return pltpu.make_async_remote_copy(
            src_ref=src, dst_ref=dst, send_sem=send, recv_sem=recv,
            device_id=where, device_id_type=MESH,
        )

    barrier = pltpu.get_barrier_semaphore()
    pl.semaphore_signal(barrier, inc=1, device_id={"slab": other_slab}, device_id_type=MESH)
    for step in range(1, 8):
        place = (x * 4 + z + step) % 8
        pl.semaphore_signal(
            barrier, inc=1, device_id={"row": place // 4, "col": place % 4}, device_id_type=MESH
        )
    pl.semaphore_wait(barrier, 8)

    loads = [
        pltpu.make_async_copy(trans, ops.at[0], load_sem.at[0]),
        pltpu.make_async_copy(refl, ops.at[2], load_sem.at[1]),
    ]
    for copy in loads:
        copy.start()

    def shot_block(b, c):
        return shots.at[pl.ds(pl.multiple_of(b * depth, depth), depth), pl.ds(pl.multiple_of(c * lanes, lanes), lanes)]

    def outer(j, at):
        return at if j == 0 else 1 - at

    def cross(j):
        return remote(
            shot_block(outer(j, x), other_x), inbox.at[j], cross_send.at[j], cross_recv.at[j],
            row=other_x,
        )

    def near_home():
        return remote(
            shot_block(z % 2, x), faces.at[z, x], face_send.at[0, z], face_recv.at[0, z],
            row=other_x,
        )

    home_load = pltpu.make_async_copy(
        shot_block(z % 2, other_x), faces.at[z, other_x], home_sem.at[0]
    )

    def hand_on(source, b, at, to, act):
        @pl.when(to == z)
        def _():
            if act == "start":
                pltpu.make_async_copy(source, faces.at[z, x], init_recv.at[z]).start()

        @pl.when(to != z)
        def _():
            copy = remote(source, faces.at[z, x], init_send.at[at], init_recv.at[z], col=to)
            copy.start() if act == "start" else copy.wait_send()

    def own_block(j, act):
        b = outer(j, x)
        hand_on(shot_block(b, x), b, j, 2 * x + b, act)

    def crossed_block(j, act):
        hand_on(inbox.at[j], j, 2 + j, 2 * other_x + outer(j, other_x), act)

    cross(0).start()

    @pl.when(home)
    def _():
        near_home().start()
        home_load.start()

    cross(1).start()
    for j in range(2):
        own_block(j, "start")

    swaps = [
        remote(refl, ops.at[1], core_send.at[0], core_recv.at[0], slab=other_slab),
        remote(trans, ops.at[3], core_send.at[1], core_recv.at[1], slab=other_slab),
    ]
    for copy in swaps:
        copy.start()
    for b in range(2):
        cross(b).wait_recv()
        crossed_block(b, "start")

    def face_copy(p, g):
        return remote(
            faces.at[g, x], faces.at[g, x], face_send.at[p, g], face_recv.at[p, g], row=other_x
        )

    def face_wait(p, g):
        return remote(
            faces.at[g, other_x], faces.at[g, other_x], face_send.at[p, g], face_recv.at[p, g],
            row=other_x,
        ).wait_recv()

    def part_copy(p, g, j, which):
        off = turn(j)
        return remote(
            stage.at[g, off], parts.at[p % 2, g, 2 * which + off],
            part_send.at[p, g, j], part_recv.at[p, g, j], row=other_x,
        )

    def turn(j):
        return 1 - high if j == 0 else high

    def gather(g):
        pltpu.make_async_copy(faces.at[g, x], faces.at[g, x], init_recv.at[g]).wait()

        @pl.when(z != g)
        def _():
            face_copy(0, g).start()

    tile = min(depth, 512)
    per = depth // tile

    def multiply(p, g, opening):
        if opening:
            if p % 2:
                swaps[p // 2].wait_recv()
            else:
                loads[p // 2].wait()
        if p == 0:
            mine = home & (z == g)

            @pl.when(mine)
            def _():
                home_load.wait()

            @pl.when(jnp.logical_not(mine))
            def _():
                face_wait(0, g)
        else:
            face_wait(p, g)
        if p < LAST:
            if p > 0:
                for j in range(2):
                    part_copy(p - 1, g, j, x).wait_send()
                settle(p - 1, g)
            both = jnp.concatenate([faces[g, other_x], faces[g, x]], axis=1)
        else:
            both = jnp.concatenate([faces[g, 0], faces[g, 1]], axis=1)

        def body(i, block):
            inside = pl.multiple_of(i * tile, tile)
            rows = pl.multiple_of(block * depth + inside, tile)
            value = jnp.dot(
                ops[p, pl.ds(rows, tile), :], both, preferred_element_type=F32
            ).astype(BF16)
            if p < LAST:
                stage[g, block, pl.ds(inside, tile), :] = value[:, :lanes]
                parts[p % 2, g, 2 * x + block, pl.ds(inside, tile), :] = value[:, lanes:]
            else:
                parts[p % 2, g, block, pl.ds(inside, tile), :] = value[:, :lanes]
                parts[p % 2, g, 2 + block, pl.ds(inside, tile), :] = value[:, lanes:]
            return block

        for j in range(2):
            lax.fori_loop(0, per, body, turn(j) if p < LAST else j)
            if p < LAST:
                part_copy(p, g, j, x).start()
                send_block(p, g, 2 * x + turn(j))
            else:
                send_last(g, (j, 2 + j))

    def send_last(g, blocks):
        @pl.when(end & is_blk(g, 2, 3))
        def _():
            for b in blocks:
                last_far(g, b, blk(1)).start()

        @pl.when(end & is_blk(g, 1))
        def _():
            for b in blocks:
                last_near(g, b, 0, blk(1)).start()

        @pl.when(inner & is_blk(g, 0))
        def _():
            for b in blocks:
                last_near(g, b, 0, blk(0)).start()

    def send_block(p, g, block):
        for copy, k in zip(end_copies(p, g), (3, 2, 1)):
            @pl.when(end & (block == blk(k)))
            def _():
                copy.start()

        @pl.when(inner & (block == blk(0)))
        def _():
            inner_copies(p, g)[0].start()

    def block_copy(p, g, k, slot, bank, sems, to, at):
        return remote(
            parts.at[p % 2, g, blk(k)], bank.at[p % 2, g, at],
            col_send.at[p, g, slot], sems.at[p, g, at], col=blk(to),
        )

    def end_copies(p, g):
        return [
            block_copy(p, g, 3, 0, far, far_recv, 1, 0),
            block_copy(p, g, 2, 1, far, far_recv, 1, 1),
            block_copy(p, g, 1, 2, near, near_recv, 1, 0),
        ]

    def inner_copies(p, g):
        return [
            block_copy(p, g, 0, 0, near, near_recv, 0, 0),
            block_copy(p, g, 3, 1, near, near_recv, 3, 1),
            block_copy(p, g, 2, 2, near, near_recv, 2, 1),
        ]

    def last_far(g, b, to):
        return remote(
            parts.at[1, g, b], far_last.at[g, b], last_send.at[g, b, 0], last_far_recv.at[g, b],
            col=to,
        )

    def last_near(g, b, at, to):
        return remote(
            parts.at[1, g, b], near_last.at[at, b], last_send.at[g, b, 1 + at],
            last_near_recv.at[at, b], col=to,
        )

    def is_blk(g, *ks):
        hit = blk(ks[0]) == g
        for k in ks[1:]:
            hit = hit | (blk(k) == g)
        return hit

    def settle(p, g):
        @pl.when(end)
        def _():
            for copy in end_copies(p, g):
                copy.wait_send()

        @pl.when(inner)
        def _():
            for copy in inner_copies(p, g):
                copy.wait_send()

    def begin(p, g):
        if p == LAST:
            return
        for j in range(2):
            part_copy(p, g, j, other_x).wait_recv()
            send_block(p, g, 2 * other_x + turn(j))

    def merge(p, g):
        if p == LAST:
            @pl.when(inner & is_blk(g, 2, 3))
            def _():
                for b in (0, 2, 1, 3):
                    last_far(g, b, blk(1)).wait_recv()
                    parts[1, g, b] = (
                        parts[1, g, b].astype(F32) + far_last[g, b].astype(F32)
                    ).astype(BF16)
                    last_near(g, b, 1, g).start()

            return

        @pl.when(inner)
        def _():
            arrive = end_copies(p, g)
            leave = inner_copies(p, g)
            for at, k in ((0, 3), (1, 2)):
                arrive[at].wait_recv()
                parts[p % 2, g, blk(k)] = (
                    parts[p % 2, g, blk(k)].astype(F32) + far[p % 2, g, at].astype(F32)
                ).astype(BF16)
                leave[1 + at].start()

    def finish(p, g):
        if p == LAST:
            return
        for at in range(2):
            block_copy(p, g, 0, 0, near, near_recv, 0, at).wait_recv()
        total = (
            parts[p % 2, g, z].astype(F32)
            + near[p % 2, g, 0].astype(F32)
            + near[p % 2, g, 1].astype(F32)
        )
        if p == 0:
            @pl.when(home | (z != g))
            def _():
                face_copy(p, g).wait_send()
        else:
            face_copy(p, g).wait_send()
        if p == 0:
            kept[g] = total.astype(BF16)
        if p == 2:
            total = total + kept[g].astype(F32)
        faces[g, x] = total.astype(BF16)
        face_copy(p + 1, g).start()

    order = [(0, blk(g)) for g in ORDER]
    order += [(p, g) for p in range(1, LAST) for g in ORDER]
    order += [(LAST, blk(g)) for g in (3, 0, 2, 1)]
    count = len(order)

    def advance(t):
        multiply(*order[t], opening=t % 4 == 0)

    gather(order[0][1])
    advance(0)
    for t in range(1, 4):
        gather(order[t][1])
    for t in range(count + 2):
        if t in (3, 5):
            for g in ORDER[t - 3 : t - 1]:
                finish(0, g)
        if 4 <= t - 2 < count:
            finish(*order[t - 2])
        if 0 <= t - 1 < count:
            merge(*order[t - 1])
        if t < count:
            begin(*order[t])
        if t + 1 < count:
            advance(t + 1)

    def out_part(ref, h, c):
        return ref.at[pl.ds(h * depth, depth), pl.ds(c * lanes, lanes)]

    for g in range(4):
        @pl.when(z == g)
        def _():
            for b in (0, 2, 1, 3):
                for at in range(2):
                    last_near(g, b, at, z).wait_recv()
                c, h = b // 2, b % 2
                total_out[pl.ds(h * depth, depth), pl.ds(c * lanes, lanes)] = (
                    parts[1, g, b].astype(F32)
                    + near_last[0, b].astype(F32)
                    + near_last[1, b].astype(F32)
                ).astype(BF16)
                pltpu.make_async_copy(out_part(total_out, h, c), out_part(out, h, c), out_sem.at[b]).start()

    for g in range(4):
        settle(LAST - 1, g)
        face_copy(LAST, g).wait_send()
        for j in range(2):
            part_copy(LAST - 1, g, j, x).wait_send()

        @pl.when(end & is_blk(g, 2, 3))
        def _():
            for b in range(4):
                last_far(g, b, blk(1)).wait_send()

        @pl.when(end & is_blk(g, 1))
        def _():
            for b in range(4):
                last_near(g, b, 0, blk(1)).wait_send()

        @pl.when(inner & is_blk(g, 0))
        def _():
            for b in range(4):
                last_near(g, b, 0, blk(0)).wait_send()

        @pl.when(inner & is_blk(g, 2, 3))
        def _():
            for b in range(4):
                last_near(g, b, 1, jnp.int32(g)).wait_send()

    for copy in swaps:
        copy.wait_send()
    for b in range(2):
        cross(b).wait_send()
        own_block(b, "wait")
        crossed_block(b, "wait")
    for b in range(4):
        c, h = b // 2, b % 2
        pltpu.make_async_copy(out_part(total_out, h, c), out_part(out, h, c), out_sem.at[b]).wait()


def chain(reflection, transmission, shots):
    refl, trans, tile = reflection[0], transmission[0], shots[0]
    height, inner = trans.shape
    lanes = tile.shape[1] // 2
    hbm = pl.BlockSpec(memory_space=pl.ANY)
    dma = pltpu.SemaphoreType.DMA
    block = (inner, lanes)
    out = pl.pallas_call(
        chain_kernel,
        out_shape=jax.ShapeDtypeStruct(tile.shape, BF16),
        in_specs=[hbm] * 3,
        out_specs=hbm,
        scratch_shapes=[
            pltpu.VMEM(tile.shape, BF16),
            pltpu.VMEM((4, height, inner), BF16),
            pltpu.VMEM((2,) + block, BF16),
            pltpu.VMEM((4, 2) + block, BF16),
            pltpu.VMEM((4,) + block, BF16),
            pltpu.VMEM((4, 2) + block, BF16),
            pltpu.VMEM((2, 4, 4) + block, BF16),
            pltpu.VMEM((2, 4, 2) + block, BF16),
            pltpu.VMEM((2, 4, 2) + block, BF16),
            pltpu.VMEM((4, 4) + block, BF16),
            pltpu.VMEM((2, 4) + block, BF16),
            dma((2,)), dma((1,)), dma((2,)), dma((2,)), dma((2,)), dma((2,)), dma((4,)), dma((4,)),
            dma((4, 4)), dma((4, 4)), dma((3, 4, 2)), dma((3, 4, 2)),
            dma((3, 4, 3)), dma((3, 4, 2)), dma((3, 4, 2)),
            dma((4, 4, 3)), dma((4, 4)), dma((2, 4)), dma((4,)),
        ],
        compiler_params=pltpu.CompilerParams(
            collective_id=0, has_side_effects=True, vmem_limit_bytes=60 << 20
        ),
    )(refl, trans, tile)
    return out[None]


def on_slice(reflection, transmission, shots):
    height, inner = transmission.shape[1:]
    fits = (
        lax.axis_size("row") == 2
        and lax.axis_size("col") == 4
        and height == 2 * inner
        and inner % 512 == 0
        and shots.shape[2] % 256 == 0
        and 11 * height * inner < 24 << 20
    )
    if fits:
        return chain(reflection, transmission, shots)
    return on_device(reflection, transmission, shots)


def solution(mesh):
    placed = (P("slab", "row", "col"), P("slab", "row", "col"), P("slab", "row", "col"))
    return jax.shard_map(
        on_slice, mesh=mesh, in_specs=placed, out_specs=P("slab", "row", "col"), check_vma=False
    )
```

```python
import jax
import jax.numpy as jnp
from jax import lax
from jax.experimental import pallas as pl
from jax.experimental.pallas import tpu as pltpu
from jax.sharding import PartitionSpec as P

GROUPS = 2


def partner(block, axis, bit):
    count = lax.axis_size(axis)
    route = []
    for low in range(count):
        high = low | 1 << bit
        if high != low and high < count:
            route += [(low, high), (high, low)]
    return lax.ppermute(block, axis, route)


def shift(block, axis, by):
    count = lax.axis_size(axis)
    by %= count
    if by == 0:
        return block
    return lax.ppermute(block, axis, [(i, (i + by) % count) for i in range(count)])


def pick(options, place):
    chosen = options[0]
    for at in range(1, len(options)):
        chosen = jnp.where(place == at, options[at], chosen)
    return chosen


def in_order(relative, me):
    count = len(relative)
    return [pick([relative[(j - at) % count] for at in range(count)], me) for j in range(count)]


def dot(a, b):
    return jnp.dot(a, b, preferred_element_type=jnp.float32)


def on_device(reflection, transmission, shots):
    own_refl = reflection[0]
    own_trans = transmission[0]
    shot_tile = shots[0]
    rows, cols = lax.axis_size("row"), lax.axis_size("col")
    x = lax.axis_index("row")
    bf16 = jnp.bfloat16
    far_refl, far_trans = partner((own_refl, own_trans), "slab", 0)

    width = shot_tile.shape[1] // rows
    kept = []
    for k in range(rows):
        piece = lax.dynamic_slice_in_dim(shot_tile, ((x + k) % rows) * width, width, axis=1)
        kept.append(shift(piece, "row", k))
    face = jnp.concatenate(in_order([kept[-k % rows] for k in range(rows)], x), axis=0)
    depth = face.shape[0] // cols
    face = lax.all_to_all(face.reshape(cols, depth, width), "col", 0, 0)

    groups = GROUPS if cols % GROUPS == 0 else 1
    per = cols // groups
    state = []
    for g in range(groups):
        mine = jnp.concatenate([face[g * per + i] for i in range(per)], axis=1)
        state.append(mine)

    def product(operator, mine):
        pieces = [shift(mine, "row", k) for k in range(rows)]
        sent = [
            shift(dot(operator, pieces[k]).astype(bf16), "row", -k) for k in range(rows)
        ]
        whole = jnp.concatenate(in_order(sent, x), axis=0)
        return lax.psum_scatter(whole, "col", scatter_dimension=0, tiled=True)

    first = [product(own_trans, mine) for mine in state]
    middle = [product(far_refl, mine) for mine in first]
    bounce = [product(own_refl, mine) for mine in middle]
    summed = [
        (a.astype(jnp.float32) + b.astype(jnp.float32)).astype(bf16)
        for a, b in zip(first, bounce)
    ]
    panels = []
    for mine in summed:
        pieces = [shift(mine, "row", k) for k in range(rows)]
        ordered = in_order([pieces[-k % rows] for k in range(rows)], x)
        for i in range(per):
            panels.append(
                jnp.concatenate([o[:, i * width : (i + 1) * width] for o in ordered], axis=1)
            )
    merged = jnp.stack([dot(far_trans, p).astype(bf16) for p in panels])
    merged = lax.psum_scatter(merged, "col", scatter_dimension=0, tiled=True)
    return merged


F32, BF16 = jnp.float32, jnp.bfloat16
ORDER = (0, 3, 2, 1)
LAST = 3
MESH = pl.DeviceIdType.MESH


def chain_kernel(
    refl, trans, shots, out, total_out, ops, inbox, faces, kept, stage, parts, far, near, far_last, near_last,
    load_sem, home_sem, core_send, core_recv, cross_send, cross_recv, init_send, init_recv, face_send, face_recv,
    part_send, part_recv, col_send, far_recv, near_recv,
    last_send, last_far_recv, last_near_recv, out_sem,
):
    s, x, z = lax.axis_index("slab"), lax.axis_index("row"), lax.axis_index("col")
    other_slab = s + 1 - 2 * (s % 2)
    other_x = 1 - x
    height = trans.shape[0]
    depth = faces.shape[2]
    lanes = faces.shape[3]
    high = z // 2
    end = (z == 0) | (z == 3)
    inner = (z == 1) | (z == 2)
    home = x == high

    def blk(k):
        return k + high * (3 - 2 * k)

    def remote(src, dst, send, recv, **where):
        return pltpu.make_async_remote_copy(
            src_ref=src, dst_ref=dst, send_sem=send, recv_sem=recv,
            device_id=where, device_id_type=MESH,
        )

    barrier = pltpu.get_barrier_semaphore()
    pl.semaphore_signal(barrier, inc=1, device_id={"slab": other_slab}, device_id_type=MESH)
    for step in range(1, 8):
        place = (x * 4 + z + step) % 8
        pl.semaphore_signal(
            barrier, inc=1, device_id={"row": place // 4, "col": place % 4}, device_id_type=MESH
        )
    pl.semaphore_wait(barrier, 8)

    loads = [
        pltpu.make_async_copy(trans, ops.at[0], load_sem.at[0]),
        pltpu.make_async_copy(refl, ops.at[2], load_sem.at[1]),
    ]
    for copy in loads:
        copy.start()

    def shot_block(b, c):
        return shots.at[pl.ds(pl.multiple_of(b * depth, depth), depth), pl.ds(pl.multiple_of(c * lanes, lanes), lanes)]

    def outer(j, at):
        return at if j == 0 else 1 - at

    def cross(j):
        return remote(
            shot_block(outer(j, x), other_x), inbox.at[j], cross_send.at[j], cross_recv.at[j],
            row=other_x,
        )

    def near_home():
        return remote(
            shot_block(z % 2, x), faces.at[z, x], face_send.at[0, z], face_recv.at[0, z],
            row=other_x,
        )

    home_load = pltpu.make_async_copy(
        shot_block(z % 2, other_x), faces.at[z, other_x], home_sem.at[0]
    )

    def hand_on(source, b, at, to, act):
        @pl.when(to == z)
        def _():
            if act == "start":
                pltpu.make_async_copy(source, faces.at[z, x], init_recv.at[z]).start()

        @pl.when(to != z)
        def _():
            copy = remote(source, faces.at[z, x], init_send.at[at], init_recv.at[z], col=to)
            copy.start() if act == "start" else copy.wait_send()

    def own_block(j, act):
        b = outer(j, x)
        hand_on(shot_block(b, x), b, j, 2 * x + b, act)

    def crossed_block(j, act):
        hand_on(inbox.at[j], j, 2 + j, 2 * other_x + outer(j, other_x), act)

    cross(0).start()

    @pl.when(home)
    def _():
        near_home().start()
        home_load.start()

    cross(1).start()
    for j in range(2):
        own_block(j, "start")

    swaps = [
        remote(refl, ops.at[1], core_send.at[0], core_recv.at[0], slab=other_slab),
        remote(trans, ops.at[3], core_send.at[1], core_recv.at[1], slab=other_slab),
    ]
    for copy in swaps:
        copy.start()
    for b in range(2):
        cross(b).wait_recv()
        crossed_block(b, "start")

    def face_copy(p, g):
        return remote(
            faces.at[g, x], faces.at[g, x], face_send.at[p, g], face_recv.at[p, g], row=other_x
        )

    def face_wait(p, g):
        return remote(
            faces.at[g, other_x], faces.at[g, other_x], face_send.at[p, g], face_recv.at[p, g],
            row=other_x,
        ).wait_recv()

    def part_copy(p, g, j, which):
        off = turn(j)
        return remote(
            stage.at[g, off], parts.at[p % 2, g, 2 * which + off],
            part_send.at[p, g, j], part_recv.at[p, g, j], row=other_x,
        )

    def turn(j):
        return 1 - high if j == 0 else high

    def gather(g):
        pltpu.make_async_copy(faces.at[g, x], faces.at[g, x], init_recv.at[g]).wait()

        @pl.when(z != g)
        def _():
            face_copy(0, g).start()

    tile = min(depth, 512)
    per = depth // tile

    def multiply(p, g, opening):
        if opening:
            if p % 2:
                swaps[p // 2].wait_recv()
            else:
                loads[p // 2].wait()
        if p == 0:
            mine = home & (z == g)

            @pl.when(mine)
            def _():
                home_load.wait()

            @pl.when(jnp.logical_not(mine))
            def _():
                face_wait(0, g)
        else:
            face_wait(p, g)
        if p < LAST:
            if p > 0:
                for j in range(2):
                    part_copy(p - 1, g, j, x).wait_send()
                settle(p - 1, g)
            both = jnp.concatenate([faces[g, other_x], faces[g, x]], axis=1)
        else:
            both = jnp.concatenate([faces[g, 0], faces[g, 1]], axis=1)

        def body(i, block):
            inside = pl.multiple_of(i * tile, tile)
            rows = pl.multiple_of(block * depth + inside, tile)
            value = jnp.dot(
                ops[p, pl.ds(rows, tile), :], both, preferred_element_type=F32
            ).astype(BF16)
            if p < LAST:
                stage[g, block, pl.ds(inside, tile), :] = value[:, :lanes]
                parts[p % 2, g, 2 * x + block, pl.ds(inside, tile), :] = value[:, lanes:]
            else:
                parts[p % 2, g, block, pl.ds(inside, tile), :] = value[:, :lanes]
                parts[p % 2, g, 2 + block, pl.ds(inside, tile), :] = value[:, lanes:]
            return block

        for j in range(2):
            lax.fori_loop(0, per, body, turn(j) if p < LAST else j)
            if p < LAST:
                part_copy(p, g, j, x).start()
                send_block(p, g, 2 * x + turn(j))
            else:
                send_last(g, (j, 2 + j))

    def send_last(g, blocks):
        @pl.when(end & is_blk(g, 2, 3))
        def _():
            for b in blocks:
                last_far(g, b, blk(1)).start()

        @pl.when(end & is_blk(g, 1))
        def _():
            for b in blocks:
                last_near(g, b, 0, blk(1)).start()

        @pl.when(inner & is_blk(g, 0))
        def _():
            for b in blocks:
                last_near(g, b, 0, blk(0)).start()

    def send_block(p, g, block):
        for copy, k in zip(end_copies(p, g), (3, 2, 1)):
            @pl.when(end & (block == blk(k)))
            def _():
                copy.start()

        @pl.when(inner & (block == blk(0)))
        def _():
            inner_copies(p, g)[0].start()

    def block_copy(p, g, k, slot, bank, sems, to, at):
        return remote(
            parts.at[p % 2, g, blk(k)], bank.at[p % 2, g, at],
            col_send.at[p, g, slot], sems.at[p, g, at], col=blk(to),
        )

    def end_copies(p, g):
        return [
            block_copy(p, g, 3, 0, far, far_recv, 1, 0),
            block_copy(p, g, 2, 1, far, far_recv, 1, 1),
            block_copy(p, g, 1, 2, near, near_recv, 1, 0),
        ]

    def inner_copies(p, g):
        return [
            block_copy(p, g, 0, 0, near, near_recv, 0, 0),
            block_copy(p, g, 3, 1, near, near_recv, 3, 1),
            block_copy(p, g, 2, 2, near, near_recv, 2, 1),
        ]

    def last_far(g, b, to):
        return remote(
            parts.at[1, g, b], far_last.at[g, b], last_send.at[g, b, 0], last_far_recv.at[g, b],
            col=to,
        )

    def last_near(g, b, at, to):
        return remote(
            parts.at[1, g, b], near_last.at[at, b], last_send.at[g, b, 1 + at],
            last_near_recv.at[at, b], col=to,
        )

    def is_blk(g, *ks):
        hit = blk(ks[0]) == g
        for k in ks[1:]:
            hit = hit | (blk(k) == g)
        return hit

    def settle(p, g):
        @pl.when(end)
        def _():
            for copy in end_copies(p, g):
                copy.wait_send()

        @pl.when(inner)
        def _():
            for copy in inner_copies(p, g):
                copy.wait_send()

    def begin(p, g):
        if p == LAST:
            return
        for j in range(2):
            part_copy(p, g, j, other_x).wait_recv()
            send_block(p, g, 2 * other_x + turn(j))

    def merge(p, g):
        if p == LAST:
            @pl.when(inner & is_blk(g, 2, 3))
            def _():
                for b in (0, 2, 1, 3):
                    last_far(g, b, blk(1)).wait_recv()
                    parts[1, g, b] = (
                        parts[1, g, b].astype(F32) + far_last[g, b].astype(F32)
                    ).astype(BF16)
                    last_near(g, b, 1, g).start()

            return

        @pl.when(inner)
        def _():
            arrive = end_copies(p, g)
            leave = inner_copies(p, g)
            for at, k in ((1, 2), (0, 3)):
                arrive[at].wait_recv()
                parts[p % 2, g, blk(k)] = (
                    parts[p % 2, g, blk(k)].astype(F32) + far[p % 2, g, at].astype(F32)
                ).astype(BF16)
                leave[1 + at].start()

    def finish(p, g):
        if p == LAST:
            return
        for at in range(2):
            block_copy(p, g, 0, 0, near, near_recv, 0, at).wait_recv()
        total = (
            parts[p % 2, g, z].astype(F32)
            + near[p % 2, g, 0].astype(F32)
            + near[p % 2, g, 1].astype(F32)
        )
        if p == 0:
            @pl.when(home | (z != g))
            def _():
                face_copy(p, g).wait_send()
        else:
            face_copy(p, g).wait_send()
        if p == 0:
            kept[g] = total.astype(BF16)
        if p == 2:
            total = total + kept[g].astype(F32)
        faces[g, x] = total.astype(BF16)
        face_copy(p + 1, g).start()

    order = [(0, blk(g)) for g in ORDER]
    order += [(p, g) for p in range(1, LAST) for g in ORDER]
    order += [(LAST, blk(g)) for g in (3, 0, 2, 1)]
    count = len(order)

    def advance(t):
        multiply(*order[t], opening=t % 4 == 0)

    gather(order[0][1])
    advance(0)
    for t in range(1, 4):
        gather(order[t][1])
    for t in range(count + 2):
        if t in (3, 5):
            for g in ORDER[t - 3 : t - 1]:
                finish(0, g)
        if 4 <= t - 2 < count:
            finish(*order[t - 2])
        if 0 <= t - 1 < count:
            merge(*order[t - 1])
        if t < count:
            begin(*order[t])
        if t + 1 < count:
            advance(t + 1)

    def out_part(ref, h, c):
        return ref.at[pl.ds(h * depth, depth), pl.ds(c * lanes, lanes)]

    for g in range(4):
        @pl.when(z == g)
        def _():
            for b in (0, 2, 1, 3):
                for at in range(2):
                    last_near(g, b, at, z).wait_recv()
                c, h = b // 2, b % 2
                total_out[pl.ds(h * depth, depth), pl.ds(c * lanes, lanes)] = (
                    parts[1, g, b].astype(F32)
                    + near_last[0, b].astype(F32)
                    + near_last[1, b].astype(F32)
                ).astype(BF16)
                pltpu.make_async_copy(out_part(total_out, h, c), out_part(out, h, c), out_sem.at[b]).start()

    for g in range(4):
        settle(LAST - 1, g)
        face_copy(LAST, g).wait_send()
        for j in range(2):
            part_copy(LAST - 1, g, j, x).wait_send()

        @pl.when(end & is_blk(g, 2, 3))
        def _():
            for b in range(4):
                last_far(g, b, blk(1)).wait_send()

        @pl.when(end & is_blk(g, 1))
        def _():
            for b in range(4):
                last_near(g, b, 0, blk(1)).wait_send()

        @pl.when(inner & is_blk(g, 0))
        def _():
            for b in range(4):
                last_near(g, b, 0, blk(0)).wait_send()

        @pl.when(inner & is_blk(g, 2, 3))
        def _():
            for b in range(4):
                last_near(g, b, 1, jnp.int32(g)).wait_send()

    for copy in swaps:
        copy.wait_send()
    for b in range(2):
        cross(b).wait_send()
        own_block(b, "wait")
        crossed_block(b, "wait")
    for b in range(4):
        c, h = b // 2, b % 2
        pltpu.make_async_copy(out_part(total_out, h, c), out_part(out, h, c), out_sem.at[b]).wait()


def chain(reflection, transmission, shots):
    refl, trans, tile = reflection[0], transmission[0], shots[0]
    height, inner = trans.shape
    lanes = tile.shape[1] // 2
    hbm = pl.BlockSpec(memory_space=pl.ANY)
    dma = pltpu.SemaphoreType.DMA
    block = (inner, lanes)
    out = pl.pallas_call(
        chain_kernel,
        out_shape=jax.ShapeDtypeStruct(tile.shape, BF16),
        in_specs=[hbm] * 3,
        out_specs=hbm,
        scratch_shapes=[
            pltpu.VMEM(tile.shape, BF16),
            pltpu.VMEM((4, height, inner), BF16),
            pltpu.VMEM((2,) + block, BF16),
            pltpu.VMEM((4, 2) + block, BF16),
            pltpu.VMEM((4,) + block, BF16),
            pltpu.VMEM((4, 2) + block, BF16),
            pltpu.VMEM((2, 4, 4) + block, BF16),
            pltpu.VMEM((2, 4, 2) + block, BF16),
            pltpu.VMEM((2, 4, 2) + block, BF16),
            pltpu.VMEM((4, 4) + block, BF16),
            pltpu.VMEM((2, 4) + block, BF16),
            dma((2,)), dma((1,)), dma((2,)), dma((2,)), dma((2,)), dma((2,)), dma((4,)), dma((4,)),
            dma((4, 4)), dma((4, 4)), dma((3, 4, 2)), dma((3, 4, 2)),
            dma((3, 4, 3)), dma((3, 4, 2)), dma((3, 4, 2)),
            dma((4, 4, 3)), dma((4, 4)), dma((2, 4)), dma((4,)),
        ],
        compiler_params=pltpu.CompilerParams(
            collective_id=0, has_side_effects=True, vmem_limit_bytes=48 << 20
        ),
    )(refl, trans, tile)
    return out[None]


def on_slice(reflection, transmission, shots):
    height, inner = transmission.shape[1:]
    fits = (
        lax.axis_size("row") == 2
        and lax.axis_size("col") == 4
        and height == 2 * inner
        and inner % 512 == 0
        and shots.shape[2] % 256 == 0
        and 11 * height * inner < 24 << 20
    )
    if fits:
        return chain(reflection, transmission, shots)
    return on_device(reflection, transmission, shots)


def solution(mesh):
    placed = (P("slab", "row", "col"), P("slab", "row", "col"), P("slab", "row", "col"))
    return jax.shard_map(
        on_slice, mesh=mesh, in_specs=placed, out_specs=P("slab", "row", "col"), check_vma=False
    )
```
